32 devices in a mesh: grp: 4 (over y, x), row: 8 (over z, core).
Axes of the slice: x: 2, y: 2, z: 4, core: 2. Of those that a mesh axis runs over, the one named last changes fastest.
Arguments:
- matrix_tiles: float32 [128, 32, 128, 128], P(('grp', 'row')), may hold values from -2 to 2, as said below
- column_index: int32 [128, 32], P(('grp', 'row')), may hold values from 0 to 127, as said below
- precond: float32 [128, 128, 128], P(('grp', 'row')), may hold values from -12 to 16, as said below
- right_side: float32 [128, 16, 128], P(('grp', 'row')), may hold values from -60 to 60
- lost_group: int32 [1], replicated, may hold values from 0 to 16383
Outputs:
- recovered: float32 [128, 16, 128], P(('grp', 'row'))
- true_residual: float32 [128, 16, 128], P(('grp', 'row'))
The draws below stay inside these ranges and needn't reach their ends.
Inputs may be any that keep to these rules, and one draw needn't show every extreme that they name: `column_index`: entry 0 of block row i is i; entry 1 is i + 12, or i - 12 where i + 12 passes the end; every entry lies within 12 of its block row. `precond`: every block is symmetric positive definite. `matrix_tiles`: the diagonal tile of each block row is near the identity.
All inputs are finite; a program needn't handle non-finite values.
Results may differ from the reference program's by a relative error of at most 0.0003.
Values sent between devices are 32-bit elements; how exact they have to be, the bound alone decides.
No kernel may reach another device: no remote copies, remote signals or barrier semaphores. Data moves between devices by JAX's collectives and lax.ppermute only.
A program may use at most 64 MiB of HBM per device.

```python
import math
import jax
import jax.numpy as jnp
from jax import lax

TB = 128
K = 32
COLS = 16
BR = 4
OUTER = 2
INNER = 2
BAND = 12
NB = 128
N_GRP = 4
N_ROW = 8


def draw_matrix_tiles(key, part):
    shape_all = (NB, K, TB, TB)
    noise = jax.random.normal(key, shape_all, jnp.float32)
    off_scale = 0.2 / math.sqrt((K - 1) * TB)
    diag_scale = 0.15 / math.sqrt(TB)
    slots = jnp.arange(K, dtype=jnp.int32)[None, :, None, None]
    identity = jnp.eye(TB, dtype=jnp.float32)[None, None, :, :]
    return jnp.where(slots == 0, identity + diag_scale * noise, off_scale * noise)


def draw_column_index(key, part):
    key_reach, key_pick = jax.random.split(key)
    rows = jnp.arange(NB, dtype=jnp.int32)[:, None]
    reach = jax.random.randint(key_reach, (NB, 1), 1, BAND + 1, dtype=jnp.int32)
    picks = jax.random.randint(key_pick, (NB, K), 0, 1 << 20, dtype=jnp.int32)
    offsets = picks % (2 * reach + 1) - reach
    target = rows + offsets
    target = jnp.where((target < 0) | (target >= NB), rows - offsets, target)
    slots = jnp.arange(K, dtype=jnp.int32)[None, :]
    farthest = jnp.where(rows + BAND < NB, rows + BAND, rows - BAND)
    target = jnp.where(slots == 0, rows, jnp.where(slots == 1, farthest, target))
    return target.astype(jnp.int32)


def draw_precond(key, part):
    key_noise, key_scale = jax.random.split(key)
    noise = jax.random.normal(key_noise, (NB, TB, TB), jnp.float32)
    scales = jnp.exp(jax.random.uniform(key_scale, (NB, TB), jnp.float32, math.log(0.5), math.log(2.0)))
    symmetric = 0.5 * (noise + jnp.swapaxes(noise, 1, 2))
    core = jnp.eye(TB, dtype=jnp.float32)[None] + 0.3 / math.sqrt(TB) * symmetric
    return scales[:, :, None] * core * scales[:, None, :]


def draw_right_side(key, part):
    key_noise, key_cols = jax.random.split(key, 2)
    position = jnp.arange(NB, dtype=jnp.float32) / max(NB - 1, 1)
    col_scale = jnp.exp(jax.random.uniform(key_cols, (COLS,), jnp.float32, math.log(0.3), math.log(3.0)))
    noise = jax.random.normal(key_noise, (NB, COLS, TB), jnp.float32)
    rising = (1.0 + 2.0 * position) / 2.0
    return noise * rising[:, None, None] * col_scale[None, :, None]


def setup_inputs(seed: int = 0) -> dict:
    seeds = jax.random.split(jax.random.key(seed), 6)
    matrix_tiles = draw_matrix_tiles(jax.random.fold_in(seeds[5], 71), 0)
    column_index = draw_column_index(jax.random.fold_in(seeds[5], 71), 0)
    precond = draw_precond(jax.random.fold_in(seeds[5], 71), 0)
    right_side = draw_right_side(jax.random.fold_in(seeds[5], 71), 0)
    lost_group = jax.random.randint(seeds[4], (1,), 0, 4096 * N_GRP).astype(jnp.int32)
    return dict(matrix_tiles=matrix_tiles, column_index=column_index, precond=precond, right_side=right_side, lost_group=lost_group)


def inner_products(former, latter):
    return jnp.einsum('ica,ida->cd', former, latter, precision=lax.Precision.HIGHEST)

def scaled_by(vector, coeffs):
    return jnp.einsum('ica,cd->ida', vector, coeffs, precision=lax.Precision.HIGHEST)

def solve_sym(matrix, target):
    factor = jnp.linalg.cholesky(0.5 * (matrix + matrix.T))
    middle = lax.linalg.triangular_solve(factor, target, left_side=True, lower=True)
    return lax.linalg.triangular_solve(factor, middle, left_side=True, lower=True, transpose_a=True)

def products(matrix_tiles, column_index, vector, kept_mask):
    total = column_index.shape[0]
    tile_blocks = matrix_tiles.reshape(total // BR, BR, K, TB, TB)
    col_blocks = column_index.reshape(total // BR, BR, K)
    mask_blocks = kept_mask.reshape(total // BR, BR, K)

    def one_block(packed):
        tile_block, col_block, mask_block = packed
        picked = jnp.take(vector, col_block, axis=0) * mask_block[:, :, None, None]
        return jnp.einsum('ikab,ikcb->ica', tile_block, picked, precision=lax.Precision.HIGHEST)
    return lax.map(one_block, (tile_blocks, col_blocks, mask_blocks)).reshape(total, COLS, TB)

def reference(matrix_tiles, column_index, precond, right_side, lost_group):
    total = right_side.shape[0]
    group_blocks = BR * N_ROW
    all_ones = jnp.ones(column_index.shape, jnp.float32)
    row_group = (jnp.arange(total, dtype=jnp.int32) // group_blocks)[:, None]
    other_mask = (column_index // group_blocks != row_group).astype(jnp.float32)
    solution = jnp.zeros_like(right_side)
    residual = right_side
    direction = right_side
    squares = inner_products(residual, residual)
    for outer_step in range(OUTER):
        applied = products(matrix_tiles, column_index, direction, all_ones)
        advance = solve_sym(inner_products(direction, applied), squares)
        solution = solution + scaled_by(direction, advance)
        residual = residual - scaled_by(applied, advance)
        squares_next = inner_products(residual, residual)
        mixing = solve_sym(squares, squares_next)
        direction = residual + scaled_by(direction, mixing)
        squares = squares_next
    coupled = products(matrix_tiles, column_index, solution, other_mask)
    inner_target = right_side - coupled
    lost = (lost_group[0] % N_GRP).astype(jnp.int32)
    first_row = (lost * group_blocks).astype(jnp.int32)
    sub_tiles = lax.dynamic_slice_in_dim(matrix_tiles, first_row, group_blocks, 0)
    sub_cols = lax.dynamic_slice_in_dim(column_index, first_row, group_blocks, 0) - first_row
    sub_mask = ((sub_cols >= 0) & (sub_cols < group_blocks)).astype(jnp.float32)
    sub_cols = jnp.clip(sub_cols, 0, group_blocks - 1).astype(jnp.int32)
    sub_target = lax.dynamic_slice_in_dim(inner_target, first_row, group_blocks, 0)
    sub_inverse = lax.dynamic_slice_in_dim(precond, first_row, group_blocks, 0)

    def condition(vector):
        return jnp.einsum('iab,icb->ica', sub_inverse, vector, precision=lax.Precision.HIGHEST)
    estimate = jnp.zeros_like(sub_target)
    remainder = sub_target
    smoothed = condition(remainder)
    heading = smoothed
    weight = inner_products(remainder, smoothed)
    for inner_step in range(INNER):
        applied = products(sub_tiles, sub_cols, heading, sub_mask)
        advance = solve_sym(inner_products(heading, applied), weight)
        estimate = estimate + scaled_by(heading, advance)
        remainder = remainder - scaled_by(applied, advance)
        if inner_step + 1 < INNER:
            smoothed = condition(remainder)
            weight_next = inner_products(remainder, smoothed)
            heading = smoothed + scaled_by(heading, solve_sym(weight, weight_next))
            weight = weight_next
    recovered = lax.dynamic_update_slice_in_dim(solution, estimate, first_row, 0)
    true_residual = right_side - products(matrix_tiles, column_index, recovered, all_ones)
    return (recovered, true_residual)
```

```python
import jax
import jax.numpy as jnp
from jax import lax
from jax.experimental import pallas as pl
from jax.experimental.pallas import tpu as pltpu
from jax.sharding import PartitionSpec as P

BAND = 12
SLOTS = 7
HIGHEST = lax.Precision.HIGHEST
AXES = ("grp", "row")
VMEM = pltpu.VMEM
SMEM = pltpu.SMEM


def spec(space):
    return pl.BlockSpec(memory_space=space)


def params(mib):
    return pltpu.CompilerParams(vmem_limit_bytes=mib << 20)


def dot_nt(former, latter):
    return lax.dot_general(
        former, latter, (((1,), (1,)), ((), ())), precision=HIGHEST,
        preferred_element_type=jnp.float32,
    )


def dot_tn(former, latter):
    return lax.dot_general(
        former, latter, (((0,), (0,)), ((), ())), precision=HIGHEST,
        preferred_element_type=jnp.float32,
    )


def dot_nn(former, latter):
    return jnp.dot(former, latter, precision=HIGHEST, preferred_element_type=jnp.float32)


def split3(value):
    high = value.astype(jnp.bfloat16)
    rest = value - high.astype(jnp.float32)
    middle = rest.astype(jnp.bfloat16)
    low = (rest - middle.astype(jnp.float32)).astype(jnp.bfloat16)
    return high, middle, low


def build_table(pieces, flags_ref, table_ref, classes, blocks, cols):
    slot = 0
    for piece in pieces:
        for first in range(0, piece.shape[0], blocks):
            for block in range(blocks):
                value = piece[first + block]
                for k in range(classes):
                    terms = split3(value * flags_ref[k, slot])
                    for s, term in enumerate(terms):
                        table_ref[slot * blocks + block, pl.ds((3 * k + s) * cols, cols), :] = term
            slot += 1


def row_product(index_ref, table_ref, tile_ref, row, classes, cols):
    count, tb = tile_ref.shape[1], tile_ref.shape[2]
    total = None
    for k in range(0, count, 2):
        left = jnp.concatenate(
            [table_ref[index_ref[row, k]], table_ref[index_ref[row, k + 1]]], axis=1
        )
        highs, rests = [], []
        for j in (k, k + 1):
            tile = tile_ref[row, j]
            high = tile.astype(jnp.bfloat16)
            highs.append(high)
            rests.append((tile - high.astype(jnp.float32)).astype(jnp.bfloat16))
        right = jnp.concatenate(
            [jnp.concatenate(highs, axis=1), jnp.concatenate(rests, axis=1)], axis=0
        )
        part = lax.dot_general(
            left, right, (((1,), (1,)), ((), ())), preferred_element_type=jnp.float32
        )
        total = part if total is None else total + part
    total = total[:, :tb] + total[:, tb:]
    out = []
    for k in range(classes):
        base = 3 * k * cols
        out.append(
            total[base : base + cols]
            + total[base + cols : base + 2 * cols]
            + total[base + 2 * cols : base + 3 * cols]
        )
    return out


def stream(tiles_hbm, tiles, sems):
    copies = [
        pltpu.make_async_copy(tiles_hbm.at[row], tiles.at[row], sems.at[row])
        for row in range(tiles.shape[0])
    ]
    for copy in copies:
        copy.start()
    return copies


def lanes(ref):
    return jnp.concatenate([ref[i] for i in range(ref.shape[0])], axis=1)


def pack_gram(gram_ref, former, latter, scale, cols):
    gram = dot_nt(former, latter)
    if scale is not None:
        gram = gram * scale
    width = gram.shape[1]
    packed = jnp.concatenate(
        [gram[:cols], gram[cols:], jnp.zeros((cols, gram_ref.shape[2] - 2 * width), jnp.float32)],
        axis=1,
    )
    gram_ref[...] = jnp.broadcast_to(packed[None], gram_ref.shape)


def first_kernel(index_ref, flags_ref, tiles_hbm, v, sw, p1, p2, p3, parts, image, tiles, table, sems):
    blocks, cols, _ = v.shape
    copies = stream(tiles_hbm, tiles, sems)
    build_table((v, sw, p1, p2, p3), flags_ref, table, 3, blocks, cols)
    for row in range(blocks):
        copies[row].wait()
        out = row_product(index_ref, table, tiles, row, 3, cols)
        for k in range(3):
            parts[k, row] = out[k]
        image[row] = out[0] + out[1] + out[2]


def second_kernel(
    index_ref, flags_ref, tiles_hbm, right, v, sw, p1, p2, p3, parts, gram, tiles, table, sems, image
):
    blocks, cols, _ = v.shape
    copies = stream(tiles_hbm, tiles, sems)
    build_table((v, sw, p1, p2, p3), flags_ref, table, 3, blocks, cols)
    for row in range(blocks):
        copies[row].wait()
        out = row_product(index_ref, table, tiles, row, 3, cols)
        for k in range(3):
            parts[k, row] = out[k]
        image[row] = out[0] + out[1] + out[2]
    former = jnp.concatenate([lanes(right), lanes(v)], axis=0)
    latter = jnp.concatenate([former, lanes(image)], axis=0)
    pack_gram(gram, former, latter, None, cols)


def third_kernel(
    index_ref, flags_ref, tiles_hbm, precond, v, sw, p1, p2, p3, applied, smooth, lost, tiles, table, sems
):
    blocks, cols, _ = v.shape
    copies = stream(tiles_hbm, tiles, sems)
    build_table((v, sw, p1, p2, p3), flags_ref, table, 2, blocks, cols)
    mine = flags_ref[3, 0]
    for row in range(blocks):
        copies[row].wait()
        out = row_product(index_ref, table, tiles, row, 2, cols)
        applied[row] = out[0]
        lost[row] = out[0] * mine + out[1]
        smooth[row] = dot_nt(out[0], precond[row])


def fourth_kernel(
    index_ref, flags_ref, tiles_hbm, target, head, applied, v, sw, p1, p2, p3, lost, gram,
    tiles, table, sems, second,
):
    blocks, cols, _ = v.shape
    copies = stream(tiles_hbm, tiles, sems)
    build_table((v, sw, p1, p2, p3), flags_ref, table, 2, blocks, cols)
    mine = flags_ref[3, 0]
    for row in range(blocks):
        copies[row].wait()
        out = row_product(index_ref, table, tiles, row, 2, cols)
        second[row] = out[0]
        lost[row] = out[0] * mine + out[1]
    former = jnp.concatenate([lanes(head), lanes(v)], axis=0)
    latter = jnp.concatenate([lanes(target), lanes(applied), lanes(second)], axis=0)
    pack_gram(gram, former, latter, mine, cols)


def tile_call(kernel, classes, outs, extra, tiles, operands_vmem, index, flags):
    blocks, count, tb, _ = tiles.shape
    cols = operands_vmem[-1].shape[1]
    scratch = [
        VMEM((blocks, count, tb, tb), jnp.float32),
        VMEM((SLOTS * blocks, 3 * classes * cols, tb), jnp.bfloat16),
        pltpu.SemaphoreType.DMA((blocks,)),
    ] + extra
    return pl.pallas_call(
        kernel,
        out_shape=outs,
        in_specs=[spec(SMEM), spec(SMEM), spec(pl.ANY)] + [spec(VMEM)] * len(operands_vmem),
        out_specs=[spec(VMEM)] * len(outs),
        scratch_shapes=scratch,
        compiler_params=params(32),
    )(index, flags, tiles, *operands_vmem)


def eliminate(matrix, target):
    size = matrix.shape[0]
    work = jnp.concatenate([matrix, target], axis=1)
    rows = lax.broadcasted_iota(jnp.int32, (size, 1), 0)
    for j in range(size):
        pivot = work[j : j + 1, :] / work[j : j + 1, j : j + 1]
        column = work[:, j : j + 1]
        work = jnp.where(rows == j, pivot, work - column * pivot)
    return work[:, size:]


def coefficients(gathered, cols):
    packed = jnp.sum(gathered[...], axis=0)
    width = 3 * cols
    top, bottom = packed[:, :width], packed[:, width : 2 * width]
    g00, g01 = top[:, :cols], top[:, cols : 2 * cols]
    g11 = bottom[:, cols : 2 * cols]
    big = jnp.concatenate([top[:, cols:], bottom[:, cols:]], axis=0)
    unit = (
        lax.broadcasted_iota(jnp.int32, (cols, cols), 0)
        == lax.broadcasted_iota(jnp.int32, (cols, cols), 1)
    ).astype(jnp.float32)
    g00 = 0.5 * (g00 + g00.T)
    advance = eliminate(0.5 * (g01 + g01.T), g00)
    inverse = eliminate(g00, unit)
    crossed = dot_nn(g01, advance)
    squares = g00 - crossed - crossed.T + dot_tn(advance, dot_nn(g11, advance))
    mixing = dot_nn(inverse, squares)
    heading = jnp.concatenate([unit + mixing, -advance], axis=0)
    curvature = dot_tn(heading, dot_nn(big, heading))
    second = eliminate(0.5 * (curvature + curvature.T), squares)
    combo = dot_nn(heading, second)
    return jnp.concatenate([combo[:cols] + advance, combo[cols:]], axis=0)


def outer_kernel(
    flags_ref, gathered, right, image, parts_b, parts_y, precond, solution, target, head, kept
):
    blocks, cols, tb = right.shape
    mine = flags_ref[3, 0]
    weights = coefficients(gathered, cols)

    def basis(pick):
        return jnp.concatenate(
            [
                jnp.concatenate([pick(0, i) for i in range(blocks)], axis=1),
                jnp.concatenate([pick(1, i) for i in range(blocks)], axis=1),
            ],
            axis=0,
        )

    parts = (parts_b, parts_y)
    own = (right, image)
    stacked = jnp.concatenate(
        [
            basis(lambda n, i: own[n][i]),
            basis(lambda n, i: parts[n][1, i] + parts[n][2, i]),
            basis(lambda n, i: parts[n][0, i] * (1.0 - mine) + parts[n][2, i]),
        ],
        axis=1,
    )
    made = dot_tn(weights, stacked)
    span = blocks * tb
    for i in range(blocks):
        solution[i] = made[:, i * tb : (i + 1) * tb]
        aim = right[i] - made[:, span + i * tb : span + (i + 1) * tb]
        target[i] = aim
        head[i] = dot_nt(aim, precond[i])
        kept[i] = made[:, 2 * span + i * tb : 2 * span + (i + 1) * tb]


def inner_kernel(
    flags_ref, gathered, right, solution, kept, head, smooth, lost0, lost1, recovered, residual
):
    blocks, cols, tb = right.shape
    mine = flags_ref[3, 0]
    weights = coefficients(gathered, cols)
    stacked = jnp.concatenate(
        [
            jnp.concatenate([lanes(head), lanes(lost0)], axis=1),
            jnp.concatenate([lanes(smooth), lanes(lost1)], axis=1),
        ],
        axis=0,
    )
    made = dot_tn(weights, stacked)
    span = blocks * tb
    for i in range(blocks):
        estimate = made[:, i * tb : (i + 1) * tb]
        recovered[i] = jnp.where(mine > 0.5, estimate, solution[i])
        residual[i] = right[i] - kept[i] - made[:, span + i * tb : span + (i + 1) * tb]


def small_call(kernel, outs, flags, gathered, *arrays):
    return pl.pallas_call(
        kernel,
        out_shape=outs,
        in_specs=[spec(SMEM)] + [spec(VMEM)] * (1 + len(arrays)),
        out_specs=[spec(VMEM)] * len(outs),
        compiler_params=params(16),
    )(flags, gathered, *arrays)


def move(value, total, where):
    pairs = [(i, where(i)) for i in range(total) if 0 <= where(i) < total]
    return lax.ppermute(value, AXES, pairs)


def window(value, total):
    swapped = move(value, total, lambda i: i ^ 1)
    far = move(value, total, lambda i: i - 3 if i % 2 == 0 else i + 3)
    pair = jnp.concatenate([value, swapped], axis=0)
    near = move(pair, total, lambda i: i - 1 if i % 2 == 0 else i + 1)
    other = move(near, total, lambda i: i ^ 1)
    return value, swapped, near, other, far


def slot_offsets(odd):
    even_slots = jnp.array([0, 1, -1, -2, 2, 3, -3], jnp.int32)
    return jnp.where(odd, -even_slots, even_slots)


def exchange(gram):
    return lax.all_to_all(gram, AXES, 0, 0)


def per_device(matrix_tiles, column_index, precond, right_side, lost_group):
    blocks, cols, tb = right_side.shape
    assert -(-BAND // blocks) * 2 + 1 == SLOTS
    row_count = lax.axis_size("row")
    group_count = lax.axis_size("grp")
    total = row_count * group_count
    me = lax.axis_index(AXES)
    my_group = lax.axis_index("grp")
    lost = lost_group[0] % group_count
    mine = my_group == lost

    offsets = slot_offsets(me % 2 == 1)
    device = column_index // blocks - me
    signed = jnp.where(me % 2 == 1, -device, device)
    slot = jnp.zeros_like(signed)
    for place, offset in enumerate((0, 1, -1, -2, 2, 3, -3)):
        slot = jnp.where(signed == offset, place, slot)
    index = slot * blocks + column_index % blocks
    owner = (me + offsets) // row_count
    in_own = owner == my_group
    in_lost = owner == lost
    flags = jnp.stack(
        [
            in_own,
            jnp.logical_and(in_lost, jnp.logical_not(in_own)),
            jnp.logical_not(jnp.logical_or(in_own, in_lost)),
            jnp.broadcast_to(mine, (SLOTS,)),
        ]
    ).astype(jnp.float32)

    vec = jax.ShapeDtypeStruct(right_side.shape, jnp.float32)
    vec3 = jax.ShapeDtypeStruct((3,) + right_side.shape, jnp.float32)
    gram = jax.ShapeDtypeStruct((total, cols, tb), jnp.float32)
    held = VMEM(right_side.shape, jnp.float32)

    parts_b, image = tile_call(
        first_kernel, 3, [vec3, vec], [], matrix_tiles, window(right_side, total), index, flags
    )
    parts_y, gram_outer = tile_call(
        second_kernel, 3, [vec3, gram], [held], matrix_tiles,
        (right_side,) + window(image, total), index, flags,
    )
    solution, target, head, kept = small_call(
        outer_kernel, [vec] * 4, flags, exchange(gram_outer), right_side, image, parts_b, parts_y, precond
    )
    applied, smooth, lost0 = tile_call(
        third_kernel, 2, [vec] * 3, [], matrix_tiles, (precond,) + window(head, total), index, flags
    )
    lost1, gram_inner = tile_call(
        fourth_kernel, 2, [vec, gram], [held], matrix_tiles,
        (target, head, applied) + window(smooth, total), index, flags,
    )
    recovered, residual = small_call(
        inner_kernel, [vec] * 2, flags, exchange(gram_inner), right_side, solution, kept, head, smooth,
        lost0, lost1,
    )
    return (recovered, residual)


def solution(mesh):
    in_specs = (
        P(("grp", "row"), None, None, None),
        P(("grp", "row"), None),
        P(("grp", "row"), None, None),
        P(("grp", "row"), None, None),
        P(),
    )
    out_specs = (P(("grp", "row"), None, None), P(("grp", "row"), None, None))
    return jax.shard_map(
        per_device, mesh=mesh, in_specs=in_specs, out_specs=out_specs, check_vma=False
    )
```

```python
import jax
import jax.numpy as jnp
from jax import lax
from jax.experimental import pallas as pl
from jax.experimental.pallas import tpu as pltpu
from jax.sharding import PartitionSpec as P


BAND = 12
SLOTS = 7
HIGHEST = lax.Precision.HIGHEST
AXES = ("grp", "row")
VMEM = pltpu.VMEM
SMEM = pltpu.SMEM


def spec(space):
    return pl.BlockSpec(memory_space=space)


def params(mib):
    return pltpu.CompilerParams(vmem_limit_bytes=mib << 20)


def dot_nt(former, latter):
    return lax.dot_general(
        former, latter, (((1,), (1,)), ((), ())), precision=HIGHEST,
        preferred_element_type=jnp.float32,
    )


def dot_tn(former, latter):
    return lax.dot_general(
        former, latter, (((0,), (0,)), ((), ())), precision=HIGHEST,
        preferred_element_type=jnp.float32,
    )


def dot_nn(former, latter):
    return jnp.dot(former, latter, precision=HIGHEST, preferred_element_type=jnp.float32)


def split3(value):
    high = value.astype(jnp.bfloat16)
    rest = value - high.astype(jnp.float32)
    middle = rest.astype(jnp.bfloat16)
    low = (rest - middle.astype(jnp.float32)).astype(jnp.bfloat16)
    return high, middle, low


def build_table(pieces, flags_ref, table_ref, classes, blocks, cols):
    slot = 0
    for piece in pieces:
        for first in range(0, piece.shape[0], blocks):
            for block in range(blocks):
                value = piece[first + block]
                for k in range(classes):
                    terms = split3(value * flags_ref[k, slot])
                    for s, term in enumerate(terms):
                        table_ref[slot * blocks + block, pl.ds((3 * k + s) * cols, cols), :] = term
            slot += 1


def row_product(index_ref, table_ref, split_ref, row, classes, cols):
    pairs, tb = split_ref.shape[1], split_ref.shape[2] // 2
    total = None
    for pair in range(pairs):
        left = jnp.concatenate(
            [table_ref[index_ref[row, 2 * pair]], table_ref[index_ref[row, 2 * pair + 1]]], axis=1
        )
        part = lax.dot_general(
            left, split_ref[row, pair], (((1,), (1,)), ((), ())),
            preferred_element_type=jnp.float32,
        )
        total = part if total is None else total + part
    total = total[:, :tb] + total[:, tb:]
    out = []
    for k in range(classes):
        base = 3 * k * cols
        out.append(
            total[base : base + cols]
            + total[base + cols : base + 2 * cols]
            + total[base + 2 * cols : base + 3 * cols]
        )
    return out


def split_kernel(tiles_hbm, split, tiles, sems):
    blocks, count, tb, _ = tiles.shape
    copies = [
        pltpu.make_async_copy(tiles_hbm.at[row], tiles.at[row], sems.at[row])
        for row in range(blocks)
    ]
    for copy in copies:
        copy.start()
    for row in range(blocks):
        copies[row].wait()
        for k in range(count):
            tile = tiles[row, k]
            high = tile.astype(jnp.bfloat16)
            rest = (tile - high.astype(jnp.float32)).astype(jnp.bfloat16)
            side = (k % 2) * tb
            split[row, k // 2, 0:tb, side : side + tb] = high
            split[row, k // 2, tb : 2 * tb, side : side + tb] = rest


def split_call(tiles):
    blocks, count, tb, _ = tiles.shape
    return pl.pallas_call(
        split_kernel,
        out_shape=jax.ShapeDtypeStruct((blocks, count // 2, 2 * tb, 2 * tb), jnp.bfloat16),
        in_specs=[spec(pltpu.HBM)],
        out_specs=spec(VMEM),
        scratch_shapes=[VMEM(tiles.shape, jnp.float32), pltpu.SemaphoreType.DMA((blocks,))],
        compiler_params=params(24),
        cost_estimate=pl.CostEstimate(flops=0, bytes_accessed=12 * tiles.size // 2, transcendentals=0),
    )(pltpu.with_memory_space_constraint(tiles, pltpu.HBM))


def lanes(ref):
    return jnp.concatenate([ref[i] for i in range(ref.shape[0])], axis=1)


def grid16(cols):
    rows = lax.broadcasted_iota(jnp.int32, (cols, cols), 0)
    columns = lax.broadcasted_iota(jnp.int32, (cols, cols), 1)
    return rows, columns


def pack_gram(gram_ref, former, latter, scale, cols):
    gram = dot_nt(former, latter)
    if scale is not None:
        gram = gram * scale
    g00, g01, g02 = (gram[:cols, k * cols : (k + 1) * cols] for k in range(3))
    g11, g12 = (gram[cols:, k * cols : (k + 1) * cols] for k in (1, 2))
    rows, columns = grid16(cols)
    upper = rows <= columns
    first = jnp.where(upper, g00, g11)
    middle = jnp.sum(jnp.where(rows == columns, g11, 0.0), axis=1, keepdims=True)
    last = jnp.where(rows == columns + 1, middle, 0.0)
    last = jnp.where((rows == cols - 1) & (columns == 0), g11[0:1, 0:1], last)
    last = jnp.where(upper, 0.5 * (g12 + g12.T), last)
    flat = jnp.concatenate([first, g01, g02, last], axis=1)
    half = cols // 2
    packed = jnp.concatenate([flat[:half], flat[half:]], axis=1)
    gram_ref[...] = jnp.broadcast_to(packed[None], gram_ref.shape)


def unpack_gram(packed, cols):
    width = packed.shape[1] // 2
    flat = jnp.concatenate([packed[:, :width], packed[:, width:]], axis=0)
    first, g01, g02, last = (flat[:, k * cols : (k + 1) * cols] for k in range(4))
    rows, columns = grid16(cols)
    above, below, diagonal = rows < columns, rows > columns, rows == columns
    g00 = jnp.where(rows <= columns, first, 0.0) + jnp.where(above, first, 0.0).T
    middle = jnp.sum(jnp.where(rows == columns + 1, last, 0.0), axis=1, keepdims=True)
    middle = jnp.where(rows == 0, last[cols - 1 : cols, 0:1], middle)
    lower = jnp.where(below, first, 0.0)
    g11 = lower + lower.T + jnp.where(diagonal, middle, 0.0)
    g12 = jnp.where(rows <= columns, last, 0.0) + jnp.where(above, last, 0.0).T
    return g00, g01, g02, g11, g12


def first_kernel(index_ref, flags_ref, split, v, sw, p1, p2, p3, parts, image, table):
    blocks, cols, _ = v.shape
    build_table((v, sw, p1, p2, p3), flags_ref, table, 3, blocks, cols)
    for row in range(blocks):
        out = row_product(index_ref, table, split, row, 3, cols)
        for k in range(3):
            parts[k, row] = out[k]
        image[row] = out[0] + out[1] + out[2]


def second_kernel(
    index_ref, flags_ref, split, right, v, sw, p1, p2, p3, parts, gram, table, image
):
    blocks, cols, _ = v.shape
    build_table((v, sw, p1, p2, p3), flags_ref, table, 3, blocks, cols)
    for row in range(blocks):
        out = row_product(index_ref, table, split, row, 3, cols)
        for k in range(3):
            parts[k, row] = out[k]
        image[row] = out[0] + out[1] + out[2]
    former = jnp.concatenate([lanes(right), lanes(v)], axis=0)
    latter = jnp.concatenate([former, lanes(image)], axis=0)
    pack_gram(gram, former, latter, None, cols)


def third_kernel(
    index_ref, flags_ref, split, precond, v, sw, p1, p2, p3, applied, smooth, lost, table
):
    blocks, cols, _ = v.shape
    build_table((v, sw, p1, p2, p3), flags_ref, table, 2, blocks, cols)
    mine = flags_ref[3, 0]
    for row in range(blocks):
        out = row_product(index_ref, table, split, row, 2, cols)
        applied[row] = out[0]
        lost[row] = out[0] * mine + out[1]
        smooth[row] = dot_nt(out[0], precond[row])


def fourth_kernel(
    index_ref, flags_ref, split, target, head, applied, v, sw, p1, p2, p3, lost, gram,
    table, second,
):
    blocks, cols, _ = v.shape
    build_table((v, sw, p1, p2, p3), flags_ref, table, 2, blocks, cols)
    mine = flags_ref[3, 0]
    for row in range(blocks):
        out = row_product(index_ref, table, split, row, 2, cols)
        second[row] = out[0]
        lost[row] = out[0] * mine + out[1]
    former = jnp.concatenate([lanes(head), lanes(v)], axis=0)
    latter = jnp.concatenate([lanes(target), lanes(applied), lanes(second)], axis=0)
    pack_gram(gram, former, latter, mine, cols)


def tile_call(kernel, classes, outs, extra, split, operands_vmem, index, flags):
    blocks, cols, tb = operands_vmem[-1].shape
    scratch = [VMEM((SLOTS * blocks, 3 * classes * cols, tb), jnp.bfloat16)] + extra
    return pl.pallas_call(
        kernel,
        out_shape=outs,
        in_specs=[spec(SMEM), spec(SMEM)] + [spec(VMEM)] * (1 + len(operands_vmem)),
        out_specs=[spec(VMEM)] * len(outs),
        scratch_shapes=scratch,
        compiler_params=params(16),
    )(index, flags, split, *operands_vmem)


def eliminate(matrix, target):
    size = matrix.shape[0]
    work = jnp.concatenate([matrix, target], axis=1)
    rows = lax.broadcasted_iota(jnp.int32, (size, 1), 0)
    for j in range(size):
        pivot = work[j : j + 1, :] / work[j : j + 1, j : j + 1]
        column = work[:, j : j + 1]
        work = jnp.where(rows == j, pivot, work - column * pivot)
    return work[:, size:]


def coefficients(gathered, cols):
    g00, g01, g02, g11, g12 = unpack_gram(jnp.sum(gathered[...], axis=0), cols)
    big = jnp.concatenate(
        [jnp.concatenate([g01, g02], axis=1), jnp.concatenate([g11, g12], axis=1)], axis=0
    )
    rows, columns = grid16(cols)
    unit = (rows == columns).astype(jnp.float32)
    advance = eliminate(0.5 * (g01 + g01.T), g00)
    inverse = eliminate(g00, unit)
    crossed = dot_nn(g01, advance)
    squares = g00 - crossed - crossed.T + dot_tn(advance, dot_nn(g11, advance))
    mixing = dot_nn(inverse, squares)
    heading = jnp.concatenate([unit + mixing, -advance], axis=0)
    curvature = dot_tn(heading, dot_nn(big, heading))
    second = eliminate(0.5 * (curvature + curvature.T), squares)
    combo = dot_nn(heading, second)
    return jnp.concatenate([combo[:cols] + advance, combo[cols:]], axis=0)


def outer_kernel(
    flags_ref, gathered, right, image, parts_b, parts_y, precond, solution, target, head, kept
):
    blocks, cols, tb = right.shape
    mine = flags_ref[3, 0]
    weights = coefficients(gathered, cols)

    def basis(pick):
        return jnp.concatenate(
            [
                jnp.concatenate([pick(0, i) for i in range(blocks)], axis=1),
                jnp.concatenate([pick(1, i) for i in range(blocks)], axis=1),
            ],
            axis=0,
        )

    parts = (parts_b, parts_y)
    own = (right, image)
    stacked = jnp.concatenate(
        [
            basis(lambda n, i: own[n][i]),
            basis(lambda n, i: parts[n][1, i] + parts[n][2, i]),
            basis(lambda n, i: parts[n][0, i] * (1.0 - mine) + parts[n][2, i]),
        ],
        axis=1,
    )
    made = dot_tn(weights, stacked)
    span = blocks * tb
    for i in range(blocks):
        solution[i] = made[:, i * tb : (i + 1) * tb]
        aim = right[i] - made[:, span + i * tb : span + (i + 1) * tb]
        target[i] = aim
        head[i] = dot_nt(aim, precond[i])
        kept[i] = made[:, 2 * span + i * tb : 2 * span + (i + 1) * tb]


def inner_kernel(
    flags_ref, gathered, right, solution, kept, head, smooth, lost0, lost1, recovered, residual
):
    blocks, cols, tb = right.shape
    mine = flags_ref[3, 0]
    weights = coefficients(gathered, cols)
    stacked = jnp.concatenate(
        [
            jnp.concatenate([lanes(head), lanes(lost0)], axis=1),
            jnp.concatenate([lanes(smooth), lanes(lost1)], axis=1),
        ],
        axis=0,
    )
    made = dot_tn(weights, stacked)
    span = blocks * tb
    for i in range(blocks):
        estimate = made[:, i * tb : (i + 1) * tb]
        recovered[i] = jnp.where(mine > 0.5, estimate, solution[i])
        residual[i] = right[i] - kept[i] - made[:, span + i * tb : span + (i + 1) * tb]


def small_call(kernel, outs, flags, gathered, *arrays):
    return pl.pallas_call(
        kernel,
        out_shape=outs,
        in_specs=[spec(SMEM)] + [spec(VMEM)] * (1 + len(arrays)),
        out_specs=[spec(VMEM)] * len(outs),
        compiler_params=params(16),
    )(flags, gathered, *arrays)


def move(value, total, where):
    pairs = [(i, where(i)) for i in range(total) if 0 <= where(i) < total]
    return lax.ppermute(value, AXES, pairs)


def window(value, total):
    swapped = move(value, total, lambda i: i ^ 1)
    pair = jnp.concatenate([value, swapped], axis=0)
    near = move(pair, total, lambda i: i - 1 if i % 2 == 0 else i + 1)
    far = move(value, total, lambda i: i - 3 if i % 2 == 0 else i + 3)
    other = move(near, total, lambda i: i ^ 1)
    return value, swapped, near, other, far


def slot_offsets(odd):
    even_slots = jnp.array([0, 1, -1, -2, 2, 3, -3], jnp.int32)
    return jnp.where(odd, -even_slots, even_slots)


def exchange(gram):
    return lax.all_to_all(gram, AXES, 0, 0)


def per_device(matrix_tiles, column_index, precond, right_side, lost_group):
    blocks, cols, tb = right_side.shape
    assert -(-BAND // blocks) * 2 + 1 == SLOTS
    row_count = lax.axis_size("row")
    group_count = lax.axis_size("grp")
    total = row_count * group_count
    me = lax.axis_index(AXES)
    my_group = lax.axis_index("grp")
    lost = lost_group[0] % group_count
    mine = my_group == lost

    offsets = slot_offsets(me % 2 == 1)
    device = column_index // blocks - me
    signed = jnp.where(me % 2 == 1, -device, device)
    slot = jnp.zeros_like(signed)
    for place, offset in enumerate((0, 1, -1, -2, 2, 3, -3)):
        slot = jnp.where(signed == offset, place, slot)
    index = slot * blocks + column_index % blocks
    owner = (me + offsets) // row_count
    in_own = owner == my_group
    in_lost = owner == lost
    flags = jnp.stack(
        [
            in_own,
            jnp.logical_and(in_lost, jnp.logical_not(in_own)),
            jnp.logical_not(jnp.logical_or(in_own, in_lost)),
            jnp.broadcast_to(mine, (SLOTS,)),
        ]
    ).astype(jnp.float32)

    vec = jax.ShapeDtypeStruct(right_side.shape, jnp.float32)
    vec3 = jax.ShapeDtypeStruct((3,) + right_side.shape, jnp.float32)
    gram = jax.ShapeDtypeStruct((total, cols // 2, 8 * cols), jnp.float32)
    assert tb == 8 * cols
    held = VMEM(right_side.shape, jnp.float32)

    split = split_call(matrix_tiles)
    parts_b, image = tile_call(
        first_kernel, 3, [vec3, vec], [], split, window(right_side, total), index, flags
    )
    parts_y, gram_outer = tile_call(
        second_kernel, 3, [vec3, gram], [held], split,
        (right_side,) + window(image, total), index, flags,
    )
    solution, target, head, kept = small_call(
        outer_kernel, [vec] * 4, flags, exchange(gram_outer), right_side, image, parts_b, parts_y, precond
    )
    applied, smooth, lost0 = tile_call(
        third_kernel, 2, [vec] * 3, [], split, (precond,) + window(head, total), index, flags
    )
    lost1, gram_inner = tile_call(
        fourth_kernel, 2, [vec, gram], [held], split,
        (target, head, applied) + window(smooth, total), index, flags,
    )
    recovered, residual = small_call(
        inner_kernel, [vec] * 2, flags, exchange(gram_inner), right_side, solution, kept, head, smooth,
        lost0, lost1,
    )
    return (recovered, residual)


def solution(mesh):
    in_specs = (
        P(("grp", "row"), None, None, None),
        P(("grp", "row"), None),
        P(("grp", "row"), None, None),
        P(("grp", "row"), None, None),
        P(),
    )
    out_specs = (P(("grp", "row"), None, None), P(("grp", "row"), None, None))

    return jax.shard_map(
        per_device, mesh=mesh, in_specs=in_specs, out_specs=out_specs, check_vma=False
    )
```

```python
import jax
import jax.numpy as jnp
from jax import lax
from jax.experimental import pallas as pl
from jax.experimental.pallas import tpu as pltpu
from jax.sharding import PartitionSpec as P


BAND = 12
OFFSETS = (0, 1, -1, -2, 2, 3, -3)
REACH = 3
SLOTS = len(OFFSETS)
HIGHEST = lax.Precision.HIGHEST
AXES = ("grp", "row")
VMEM = pltpu.VMEM
SMEM = pltpu.SMEM


def spec(space):
    return pl.BlockSpec(memory_space=space)


def params(mib):
    return pltpu.CompilerParams(vmem_limit_bytes=mib << 20)


def dot_nt(former, latter):
    return lax.dot_general(
        former, latter, (((1,), (1,)), ((), ())), precision=HIGHEST,
        preferred_element_type=jnp.float32,
    )


def dot_tn(former, latter):
    return lax.dot_general(
        former, latter, (((0,), (0,)), ((), ())), precision=HIGHEST,
        preferred_element_type=jnp.float32,
    )


def dot_nn(former, latter):
    return jnp.dot(former, latter, precision=HIGHEST, preferred_element_type=jnp.float32)


def split3(value):
    high = value.astype(jnp.bfloat16)
    rest = value - high.astype(jnp.float32)
    middle = rest.astype(jnp.bfloat16)
    low = (rest - middle.astype(jnp.float32)).astype(jnp.bfloat16)
    return high, middle, low


def build_table(pieces, place, table_ref, classes, blocks, cols):
    slot = 0
    for piece in pieces:
        for first in range(0, piece.shape[0], blocks):
            position, flags = place.slot(slot)
            for block in range(blocks):
                value = piece[first + block]
                for k in range(classes):
                    terms = split3(value * flags[k])
                    for s, term in enumerate(terms):
                        rows = pl.ds((3 * k + s) * cols, cols)
                        table_ref[position * blocks + block, rows, :] = term
            slot += 1


class Place:
    def __init__(self, lost_ref):
        self.me = lax.axis_index(AXES)
        self.row = lax.axis_index("row")
        self.group = lax.axis_index("grp")
        self.rows = lax.axis_size("row")
        self.lost = lax.rem(lost_ref[0], lax.axis_size("grp"))
        self.sign = 1 - 2 * lax.rem(self.me, 2)
        self.mine = jnp.where(self.group == self.lost, 1.0, 0.0)

    def slot(self, slot):
        offset = self.sign * OFFSETS[slot]
        row = self.row + offset
        side = jnp.where(row < 0, -1, jnp.where(row >= self.rows, 1, 0))
        own = jnp.where(side == 0, 1.0, 0.0)
        lost = jnp.where((side != 0) & (self.group + side == self.lost), 1.0, 0.0)
        return offset + REACH, (own, lost, 1.0 - own - lost)

    def base(self, blocks):
        return (self.me - REACH) * blocks


def row_product(columns_ref, base, table_ref, split_ref, row, classes, cols):
    pairs, tb = split_ref.shape[1], split_ref.shape[2] // 2
    total = None
    for pair in range(pairs):
        left = jnp.concatenate(
            [table_ref[columns_ref[row, 2 * pair + j] - base] for j in (0, 1)], axis=1
        )
        part = lax.dot_general(
            left, split_ref[row, pair], (((1,), (1,)), ((), ())),
            preferred_element_type=jnp.float32,
        )
        total = part if total is None else total + part
    total = total[:, :tb] + total[:, tb:]
    out = []
    for k in range(classes):
        base = 3 * k * cols
        out.append(
            total[base : base + cols]
            + total[base + cols : base + 2 * cols]
            + total[base + 2 * cols : base + 3 * cols]
        )
    return out


def split_kernel(tiles_hbm, precond, split, halves, tiles, sems):
    blocks, count, tb, _ = tiles.shape
    copies = [
        pltpu.make_async_copy(tiles_hbm.at[row], tiles.at[row], sems.at[row])
        for row in range(blocks)
    ]
    for copy in copies:
        copy.start()
    for row in range(blocks):
        high = precond[row].astype(jnp.bfloat16)
        halves[row, 0:tb] = high
        halves[row, tb : 2 * tb] = (precond[row] - high.astype(jnp.float32)).astype(jnp.bfloat16)
    for row in range(blocks):
        copies[row].wait()
        for k in range(count):
            tile = tiles[row, k]
            high = tile.astype(jnp.bfloat16)
            rest = (tile - high.astype(jnp.float32)).astype(jnp.bfloat16)
            side = (k % 2) * tb
            split[row, k // 2, 0:tb, side : side + tb] = high
            split[row, k // 2, tb : 2 * tb, side : side + tb] = rest


def split_call(tiles, precond):
    blocks, count, tb, _ = tiles.shape
    return pl.pallas_call(
        split_kernel,
        out_shape=[
            jax.ShapeDtypeStruct((blocks, count // 2, 2 * tb, 2 * tb), jnp.bfloat16),
            jax.ShapeDtypeStruct((blocks, 2 * tb, tb), jnp.bfloat16),
        ],
        in_specs=[spec(pltpu.HBM), spec(VMEM)],
        out_specs=[spec(VMEM)] * 2,
        scratch_shapes=[VMEM(tiles.shape, jnp.float32), pltpu.SemaphoreType.DMA((blocks,))],
        compiler_params=params(24),
        cost_estimate=pl.CostEstimate(flops=0, bytes_accessed=12 * tiles.size // 2, transcendentals=0),
    )(pltpu.with_memory_space_constraint(tiles, pltpu.HBM), precond)


def smoothed(value, halves, cols, tb):
    left = jnp.concatenate(split3(value), axis=0)
    both = lax.dot_general(
        left, halves, (((1,), (1,)), ((), ())), preferred_element_type=jnp.float32
    )
    both = both[:, :tb] + both[:, tb:]
    return both[:cols] + both[cols : 2 * cols] + both[2 * cols :]


def lanes(ref):
    return jnp.concatenate([ref[i] for i in range(ref.shape[0])], axis=1)


def grid16(cols):
    rows = lax.broadcasted_iota(jnp.int32, (cols, cols), 0)
    columns = lax.broadcasted_iota(jnp.int32, (cols, cols), 1)
    return rows, columns


def pack_gram(gram_ref, former, latter, scale, cols):
    gram = dot_nt(former, latter)
    if scale is not None:
        gram = gram * scale
    g00, g01, g02 = (gram[:cols, k * cols : (k + 1) * cols] for k in range(3))
    g11, g12 = (gram[cols:, k * cols : (k + 1) * cols] for k in (1, 2))
    rows, columns = grid16(cols)
    upper = rows <= columns
    first = jnp.where(upper, g00, g11)
    middle = jnp.sum(jnp.where(rows == columns, g11, 0.0), axis=1, keepdims=True)
    last = jnp.where(rows == columns + 1, middle, 0.0)
    last = jnp.where((rows == cols - 1) & (columns == 0), g11[0:1, 0:1], last)
    last = jnp.where(upper, 0.5 * (g12 + g12.T), last)
    flat = jnp.concatenate([first, g01, g02, last], axis=1)
    half = cols // 2
    packed = jnp.concatenate([flat[:half], flat[half:]], axis=1)
    gram_ref[...] = jnp.broadcast_to(packed[None], gram_ref.shape)


def unpack_gram(packed, cols):
    width = packed.shape[1] // 2
    flat = jnp.concatenate([packed[:, :width], packed[:, width:]], axis=0)
    turned = flat.T
    first, g01, g02, last = (flat[:, k * cols : (k + 1) * cols] for k in range(4))
    first_t, g01_t, g02_t, last_t = (turned[k * cols : (k + 1) * cols] for k in range(4))
    rows, columns = grid16(cols)
    upper = rows <= columns
    g00 = jnp.where(upper, first, first_t)
    middle = jnp.sum(jnp.where(rows == columns + 1, last, 0.0), axis=1, keepdims=True)
    middle = jnp.where(rows == 0, last[cols - 1 : cols, 0:1], middle)
    g11 = jnp.where(rows > columns, first, jnp.where(rows < columns, first_t, middle))
    g12 = jnp.where(upper, last, last_t)
    return g00, g01, g01_t, g02, g02_t, g11, g12


def first_kernel(columns_ref, lost_ref, split, v, sw, p1, p2, p3, parts, image, table):
    blocks, cols, _ = v.shape
    place = Place(lost_ref)
    base = place.base(blocks)
    build_table((v, sw, p1, p2, p3), place, table, 3, blocks, cols)
    for row in range(blocks):
        out = row_product(columns_ref, base, table, split, row, 3, cols)
        for k in range(3):
            parts[k, row] = out[k]
        image[row] = out[0] + out[1] + out[2]


def second_kernel(
    columns_ref, lost_ref, split, right, v, sw, p1, p2, p3, parts, gram, table, image
):
    blocks, cols, _ = v.shape
    place = Place(lost_ref)
    base = place.base(blocks)
    build_table((v, sw, p1, p2, p3), place, table, 3, blocks, cols)
    for row in range(blocks):
        out = row_product(columns_ref, base, table, split, row, 3, cols)
        for k in range(3):
            parts[k, row] = out[k]
        image[row] = out[0] + out[1] + out[2]
    former = jnp.concatenate([lanes(right), lanes(v)], axis=0)
    latter = jnp.concatenate([former, lanes(image)], axis=0)
    pack_gram(gram, former, latter, None, cols)


def third_kernel(
    columns_ref, lost_ref, split, precond, v, sw, p1, p2, p3, applied, smooth, lost, table
):
    blocks, cols, _ = v.shape
    place = Place(lost_ref)
    base = place.base(blocks)
    build_table((v, sw, p1, p2, p3), place, table, 2, blocks, cols)
    mine = place.mine
    for row in range(blocks):
        out = row_product(columns_ref, base, table, split, row, 2, cols)
        applied[row] = out[0]
        lost[row] = out[0] * mine + out[1]
        smooth[row] = smoothed(out[0], precond[row], cols, v.shape[2])


def fourth_kernel(
    columns_ref, lost_ref, split, target, head, applied, v, sw, p1, p2, p3, lost, gram,
    table, second,
):
    blocks, cols, _ = v.shape
    place = Place(lost_ref)
    base = place.base(blocks)
    build_table((v, sw, p1, p2, p3), place, table, 2, blocks, cols)
    mine = place.mine
    for row in range(blocks):
        out = row_product(columns_ref, base, table, split, row, 2, cols)
        second[row] = out[0]
        lost[row] = out[0] * mine + out[1]
    former = jnp.concatenate([lanes(head), lanes(v)], axis=0)
    latter = jnp.concatenate([lanes(target), lanes(applied), lanes(second)], axis=0)
    pack_gram(gram, former, latter, mine, cols)


def tile_call(kernel, classes, outs, extra, split, operands_vmem, columns, lost):
    blocks, cols, tb = operands_vmem[-1].shape
    scratch = [VMEM((SLOTS * blocks, 3 * classes * cols, tb), jnp.bfloat16)] + extra
    return pl.pallas_call(
        kernel,
        out_shape=outs,
        in_specs=[spec(SMEM), spec(SMEM)] + [spec(VMEM)] * (1 + len(operands_vmem)),
        out_specs=[spec(VMEM)] * len(outs),
        scratch_shapes=scratch,
        compiler_params=params(16),
    )(columns, lost, split, *operands_vmem)


def eliminate(matrix, target):
    size = matrix.shape[0]
    rows = lax.broadcasted_iota(jnp.int32, target.shape, 0)
    columns = [jnp.broadcast_to(matrix[:, k : k + 1], target.shape) for k in range(size)]
    for k in range(size):
        pivot = columns[k]
        inverse = 1.0 / pivot[k : k + 1, :]
        scaled = pivot * inverse
        here = rows == k
        top = target[k : k + 1, :]
        target = jnp.where(here, top * inverse, target - scaled * top)
        for i in range(k + 1, size):
            entry = pivot[i : i + 1, :]
            columns[i] = jnp.where(here, entry * inverse, columns[i] - scaled * entry)
    return target


def coefficients(gathered, cols):
    g00, g01, g01_t, g02, g02_t, g11, g12 = unpack_gram(jnp.sum(gathered[...], axis=0), cols)
    whole, cross = 0.5 * (g01 + g01_t), 0.5 * (g02 + g11)
    cross_t = 0.5 * (g02_t + g11)
    big = jnp.concatenate(
        [jnp.concatenate([whole, cross], axis=1), jnp.concatenate([cross_t, g12], axis=1)], axis=0
    )
    rows, columns = grid16(cols)
    unit = (rows == columns).astype(jnp.float32)
    advance = eliminate(whole, g00)
    inverse = eliminate(g00, unit)
    moved = dot_nn(jnp.concatenate([g01, g11], axis=0), advance)
    squares = g00 - moved[:cols] - dot_tn(advance, g01_t - moved[cols:])
    mixing = dot_nn(inverse, squares)
    heading = jnp.concatenate([unit + mixing, -advance], axis=0)
    curvature = dot_tn(heading, dot_nn(big, heading))
    second = eliminate(curvature, squares)
    combo = dot_nn(heading, second)
    return jnp.concatenate([combo[:cols] + advance, combo[cols:]], axis=0)


def outer_kernel(
    lost_ref, gathered, right, image, parts_b, parts_y, precond, solution, target, head, kept
):
    blocks, cols, tb = right.shape
    mine = Place(lost_ref).mine
    weights = coefficients(gathered, cols)

    def basis(pick):
        return jnp.concatenate(
            [
                jnp.concatenate([pick(0, i) for i in range(blocks)], axis=1),
                jnp.concatenate([pick(1, i) for i in range(blocks)], axis=1),
            ],
            axis=0,
        )

    parts = (parts_b, parts_y)
    own = (right, image)
    stacked = jnp.concatenate(
        [
            basis(lambda n, i: own[n][i]),
            basis(lambda n, i: parts[n][1, i] + parts[n][2, i]),
            basis(lambda n, i: parts[n][0, i] * (1.0 - mine) + parts[n][2, i]),
        ],
        axis=1,
    )
    made = dot_tn(weights, stacked)
    span = blocks * tb
    for i in range(blocks):
        solution[i] = made[:, i * tb : (i + 1) * tb]
        aim = right[i] - made[:, span + i * tb : span + (i + 1) * tb]
        target[i] = aim
        head[i] = smoothed(aim, precond[i], cols, tb)
        kept[i] = made[:, 2 * span + i * tb : 2 * span + (i + 1) * tb]


def inner_kernel(
    lost_ref, gathered, right, solution, kept, head, smooth, lost0, lost1, recovered, residual
):
    blocks, cols, tb = right.shape
    mine = Place(lost_ref).mine
    weights = coefficients(gathered, cols)
    stacked = jnp.concatenate(
        [
            jnp.concatenate([lanes(head), lanes(lost0)], axis=1),
            jnp.concatenate([lanes(smooth), lanes(lost1)], axis=1),
        ],
        axis=0,
    )
    made = dot_tn(weights, stacked)
    span = blocks * tb
    for i in range(blocks):
        estimate = made[:, i * tb : (i + 1) * tb]
        recovered[i] = jnp.where(mine > 0.5, estimate, solution[i])
        residual[i] = right[i] - kept[i] - made[:, span + i * tb : span + (i + 1) * tb]


def small_call(kernel, outs, lost, gathered, *arrays):
    return pl.pallas_call(
        kernel,
        out_shape=outs,
        in_specs=[spec(SMEM)] + [spec(VMEM)] * (1 + len(arrays)),
        out_specs=[spec(VMEM)] * len(outs),
        compiler_params=params(16),
    )(lost, gathered, *arrays)


def move(value, total, where):
    pairs = [(i, where(i)) for i in range(total) if 0 <= where(i) < total]
    return lax.ppermute(value, AXES, pairs)


def window(value, total):
    swapped = move(value, total, lambda i: i ^ 1)
    pair = jnp.concatenate([value, swapped], axis=0)
    near = move(pair, total, lambda i: i - 1 if i % 2 == 0 else i + 1)
    far = move(value, total, lambda i: i - 3 if i % 2 == 0 else i + 3)
    other = move(near, total, lambda i: i ^ 1)
    return value, swapped, near, other, far


def exchange(gram):
    return lax.all_to_all(gram, AXES, 0, 0)


def per_device(matrix_tiles, column_index, precond, right_side, lost_group):
    blocks, cols, tb = right_side.shape
    assert -(-BAND // blocks) == REACH <= lax.axis_size("row")
    total = lax.axis_size("row") * lax.axis_size("grp")

    vec = jax.ShapeDtypeStruct(right_side.shape, jnp.float32)
    vec3 = jax.ShapeDtypeStruct((3,) + right_side.shape, jnp.float32)
    gram = jax.ShapeDtypeStruct((total, cols // 2, 8 * cols), jnp.float32)
    assert tb == 8 * cols
    held = VMEM(right_side.shape, jnp.float32)

    split, halves = split_call(matrix_tiles, precond)
    parts_b, image = tile_call(
        first_kernel, 3, [vec3, vec], [], split, window(right_side, total), column_index, lost_group
    )
    parts_y, gram_outer = tile_call(
        second_kernel, 3, [vec3, gram], [held], split,
        (right_side,) + window(image, total), column_index, lost_group,
    )
    solution, target, head, kept = small_call(
        outer_kernel, [vec] * 4, lost_group, exchange(gram_outer), right_side, image, parts_b, parts_y, halves
    )
    applied, smooth, lost0 = tile_call(
        third_kernel, 2, [vec] * 3, [], split, (halves,) + window(head, total), column_index, lost_group
    )
    lost1, gram_inner = tile_call(
        fourth_kernel, 2, [vec, gram], [held], split,
        (target, head, applied) + window(smooth, total), column_index, lost_group,
    )
    recovered, residual = small_call(
        inner_kernel, [vec] * 2, lost_group, exchange(gram_inner), right_side, solution, kept, head, smooth,
        lost0, lost1,
    )
    return (recovered, residual)


def solution(mesh):
    in_specs = (
        P(("grp", "row"), None, None, None),
        P(("grp", "row"), None),
        P(("grp", "row"), None, None),
        P(("grp", "row"), None, None),
        P(),
    )
    out_specs = (P(("grp", "row"), None, None), P(("grp", "row"), None, None))

    return jax.shard_map(
        per_device, mesh=mesh, in_specs=in_specs, out_specs=out_specs, check_vma=False
    )
```

```python
import jax
import jax.numpy as jnp
from jax import lax
from jax.experimental import pallas as pl
from jax.experimental.pallas import tpu as pltpu
from jax.sharding import PartitionSpec as P


BAND = 12
OFFSETS = (0, 1, -1, -2, 2, 3, -3)
REACH = 3
OWN, LOST, ELSE = range(3)
SLOTS = len(OFFSETS)
HIGHEST = lax.Precision.HIGHEST
AXES = ("grp", "row")
VMEM = pltpu.VMEM
SMEM = pltpu.SMEM


def spec(space):
    return pl.BlockSpec(memory_space=space)


def params(mib):
    return pltpu.CompilerParams(vmem_limit_bytes=mib << 20)


def dot_nt(former, latter):
    return lax.dot_general(
        former, latter, (((1,), (1,)), ((), ())), precision=HIGHEST,
        preferred_element_type=jnp.float32,
    )


def dot_tn(former, latter):
    return lax.dot_general(
        former, latter, (((0,), (0,)), ((), ())), precision=HIGHEST,
        preferred_element_type=jnp.float32,
    )


def dot_nn(former, latter):
    return jnp.dot(former, latter, precision=HIGHEST, preferred_element_type=jnp.float32)


def split3(value):
    high = value.astype(jnp.bfloat16)
    rest = value - high.astype(jnp.float32)
    middle = rest.astype(jnp.bfloat16)
    low = (rest - middle.astype(jnp.float32)).astype(jnp.bfloat16)
    return high, middle, low


def build_table(pieces, place, table_ref, classes, blocks, cols, start=0):
    for slot, (piece, first) in enumerate(pieces):
        position, flags = place.slot(slot)
        for block in range(blocks):
            entry = position * blocks + block
            value = None if piece is None else piece[first + block]
            for k, name in enumerate(classes):
                base = 3 * (start + k) * cols
                if piece is None:
                    table_ref[entry, base : base + 3 * cols, :] = jnp.zeros(
                        (3 * cols, table_ref.shape[2]), jnp.bfloat16
                    )
                    continue
                for s, term in enumerate(split3(value * flags[name])):
                    table_ref[entry, base + s * cols : base + (s + 1) * cols, :] = term


def slots(v, sw, near, other, far, blocks, skip=0):
    first = 2 * skip * blocks
    here = (v, sw) if skip == 0 else (None, None)
    return (
        (here[0], 0), (here[1], 0), (near, first), (near, first + blocks),
        (other, first), (other, first + blocks), (far, skip * blocks),
    )


class Place:
    def __init__(self, lost_ref):
        self.me = lax.axis_index(AXES)
        self.row = lax.axis_index("row")
        self.group = lax.axis_index("grp")
        self.rows = lax.axis_size("row")
        self.lost = lax.rem(lost_ref[0], lax.axis_size("grp"))
        self.sign = 1 - 2 * lax.rem(self.me, 2)
        self.mine = jnp.where(self.group == self.lost, 1.0, 0.0)

    def slot(self, slot):
        offset = self.sign * OFFSETS[slot]
        row = self.row + offset
        side = jnp.where(row < 0, -1, jnp.where(row >= self.rows, 1, 0))
        own = jnp.where(side == 0, 1.0, 0.0)
        lost = jnp.where((side != 0) & (self.group + side == self.lost), 1.0, 0.0)
        return offset + REACH, (own, lost, 1.0 - own - lost)

    def base(self, blocks):
        return (self.me - REACH) * blocks


def row_product(columns_ref, base, table_ref, split_ref, row, classes, cols):
    pairs, tb = split_ref.shape[1], split_ref.shape[2] // 2
    total = None
    for pair in range(pairs):
        left = jnp.concatenate(
            [table_ref[columns_ref[row, 2 * pair + j] - base] for j in (0, 1)], axis=1
        )
        part = lax.dot_general(
            left, split_ref[row, pair], (((1,), (0,)), ((), ())),
            preferred_element_type=jnp.float32,
        )
        total = part if total is None else total + part
    total = total[:, :tb] + total[:, tb:]
    out = []
    for k in range(classes):
        base = 3 * k * cols
        out.append(
            total[base : base + cols]
            + total[base + cols : base + 2 * cols]
            + total[base + 2 * cols : base + 3 * cols]
        )
    return out


def split_kernel(tiles_hbm, precond_hbm, split, halves, tiles, precond, sems):
    blocks, count, tb, _ = tiles.shape
    rows, columns = grid16(2 * tb)
    unit = (rows == columns).astype(jnp.bfloat16)
    copies = [
        pltpu.make_async_copy(tiles_hbm.at[row], tiles.at[row], sems.at[row])
        for row in range(blocks)
    ]
    for copy in copies:
        copy.start()
    last = pltpu.make_async_copy(precond_hbm, precond, sems.at[blocks])
    last.start()
    for row in range(blocks):
        copies[row].wait()
        for pair in range(count // 2):
            highs, rests = [], []
            for k in (2 * pair, 2 * pair + 1):
                tile = tiles[row, k]
                high = tile.astype(jnp.bfloat16)
                highs.append(high)
                rests.append((tile - high.astype(jnp.float32)).astype(jnp.bfloat16))
            both = jnp.concatenate(
                [jnp.concatenate(highs, axis=1), jnp.concatenate(rests, axis=1)], axis=0
            )
            turned = lax.dot_general(
                unit, both, (((1,), (1,)), ((), ())), preferred_element_type=jnp.float32
            )
            split[row, pair] = turned.astype(jnp.bfloat16)
    last.wait()
    for row in range(blocks):
        high = precond[row].astype(jnp.bfloat16)
        halves[row, 0:tb] = high
        halves[row, tb : 2 * tb] = (precond[row] - high.astype(jnp.float32)).astype(jnp.bfloat16)


def split_call(tiles, precond):
    blocks, count, tb, _ = tiles.shape
    return pl.pallas_call(
        split_kernel,
        out_shape=[
            jax.ShapeDtypeStruct((blocks, count // 2, 2 * tb, 2 * tb), jnp.bfloat16),
            jax.ShapeDtypeStruct((blocks, 2 * tb, tb), jnp.bfloat16),
        ],
        in_specs=[spec(pltpu.HBM)] * 2,
        out_specs=[spec(VMEM)] * 2,
        scratch_shapes=[
            VMEM(tiles.shape, jnp.float32),
            VMEM(precond.shape, jnp.float32),
            pltpu.SemaphoreType.DMA((blocks + 1,)),
        ],
        compiler_params=params(24),
        cost_estimate=pl.CostEstimate(flops=0, bytes_accessed=12 * tiles.size // 2, transcendentals=0),
    )(*(pltpu.with_memory_space_constraint(array, pltpu.HBM) for array in (tiles, precond)))


def smoothed(value, halves, cols, tb):
    left = jnp.concatenate(split3(value), axis=0)
    both = lax.dot_general(
        left, halves, (((1,), (1,)), ((), ())), preferred_element_type=jnp.float32
    )
    both = both[:, :tb] + both[:, tb:]
    return both[:cols] + both[cols : 2 * cols] + both[2 * cols :]


def lanes(ref):
    return jnp.concatenate([ref[i] for i in range(ref.shape[0])], axis=1)


def grid16(cols):
    rows = lax.broadcasted_iota(jnp.int32, (cols, cols), 0)
    columns = lax.broadcasted_iota(jnp.int32, (cols, cols), 1)
    return rows, columns


def pack_gram(gram_ref, former, latter, scale, cols):
    gram = dot_nt(former, latter)
    if scale is not None:
        gram = gram * scale
    g00, g01, g02 = (gram[:cols, k * cols : (k + 1) * cols] for k in range(3))
    g11, g12 = (gram[cols:, k * cols : (k + 1) * cols] for k in (1, 2))
    rows, columns = grid16(cols)
    upper = rows <= columns
    first = jnp.where(upper, g00, g11)
    middle = jnp.sum(jnp.where(rows == columns, g11, 0.0), axis=1, keepdims=True)
    last = jnp.where(rows == columns + 1, middle, 0.0)
    last = jnp.where((rows == cols - 1) & (columns == 0), g11[0:1, 0:1], last)
    last = jnp.where(upper, 0.5 * (g12 + g12.T), last)
    flat = jnp.concatenate([first, g01, g02, last], axis=1)
    half = cols // 2
    packed = jnp.concatenate([flat[:half], flat[half:]], axis=1)
    gram_ref[...] = jnp.broadcast_to(packed[None], gram_ref.shape)


def unpack_gram(packed, cols):
    width = packed.shape[1] // 2
    flat = jnp.concatenate([packed[:, :width], packed[:, width:]], axis=0)
    turned = flat.T
    first, g01, g02, last = (flat[:, k * cols : (k + 1) * cols] for k in range(4))
    first_t, g01_t, g02_t, last_t = (turned[k * cols : (k + 1) * cols] for k in range(4))
    rows, columns = grid16(cols)
    upper = rows <= columns
    g00 = jnp.where(upper, first, first_t)
    middle = jnp.sum(jnp.where(rows == columns + 1, last, 0.0), axis=1, keepdims=True)
    middle = jnp.where(rows == 0, last[cols - 1 : cols, 0:1], middle)
    g11 = jnp.where(rows > columns, first, jnp.where(rows < columns, first_t, middle))
    g12 = jnp.where(upper, last, last_t)
    return g00, g01, g01_t, g02, g02_t, g11, g12


def first_kernel(columns_ref, lost_ref, split, v, sw, p1, p2, p3, parts, image, table):
    blocks, cols, _ = v.shape
    place = Place(lost_ref)
    base = place.base(blocks)
    build_table(slots(v, sw, p1, p2, p3, blocks), place, table, (OWN, LOST, ELSE), blocks, cols)
    for row in range(blocks):
        out = row_product(columns_ref, base, table, split, row, 3, cols)
        for k in range(3):
            parts[k, row] = out[k]
        image[row] = out[0] + out[1] + out[2]


def second_kernel(
    columns_ref, lost_ref, split, right, v, sw, p1, p2, p3, parts, gram, table, image
):
    blocks, cols, _ = v.shape
    place = Place(lost_ref)
    base = place.base(blocks)
    build_table(slots(v, sw, p1, p2, p3, blocks), place, table, (OWN, LOST, ELSE), blocks, cols)
    for row in range(blocks):
        out = row_product(columns_ref, base, table, split, row, 3, cols)
        for k in range(3):
            parts[k, row] = out[k]
        image[row] = out[0] + out[1] + out[2]
    former = jnp.concatenate([lanes(right), lanes(v)], axis=0)
    latter = jnp.concatenate([former, lanes(image)], axis=0)
    pack_gram(gram, former, latter, None, cols)


def third_kernel(
    columns_ref, lost_ref, split, halves, v, sw, p1, p2, p3, applied, smooth, table
):
    blocks, cols, tb = v.shape
    place = Place(lost_ref)
    base = place.base(blocks)
    build_table(slots(v, sw, p1, p2, p3, blocks), place, table, (OWN,), blocks, cols)
    for row in range(blocks):
        (applied[row],) = row_product(columns_ref, base, table, split, row, 1, cols)
    for row in range(blocks):
        smooth[row] = smoothed(applied[row], halves[row], cols, tb)


def fourth_kernel(
    columns_ref, lost_ref, split, target, head, applied, v, sw, p1, p2, p3, lost0, lost1, gram,
    table, second,
):
    blocks, cols, _ = v.shape
    place = Place(lost_ref)
    base = place.base(blocks)
    mine = place.mine
    build_table(slots(v, sw, p1, p2, p3, blocks), place, table, (OWN, LOST), blocks, cols)
    build_table(slots(v, sw, p1, p2, p3, blocks, 1), place, table, (LOST,), blocks, cols, 2)
    for row in range(blocks):
        out = row_product(columns_ref, base, table, split, row, 3, cols)
        second[row] = out[0]
        lost1[row] = out[0] * mine + out[1]
        lost0[row] = applied[row] * mine + out[2]
    former = jnp.concatenate([lanes(head), lanes(v)], axis=0)
    latter = jnp.concatenate([lanes(target), lanes(applied), lanes(second)], axis=0)
    pack_gram(gram, former, latter, mine, cols)


def tile_call(kernel, classes, outs, extra, split, operands_vmem, columns, lost):
    blocks, cols, tb = operands_vmem[-5].shape
    scratch = [VMEM((SLOTS * blocks, 3 * classes * cols, tb), jnp.bfloat16)] + extra
    return pl.pallas_call(
        kernel,
        out_shape=outs,
        in_specs=[spec(SMEM), spec(SMEM)] + [spec(VMEM)] * (1 + len(operands_vmem)),
        out_specs=[spec(VMEM)] * len(outs),
        scratch_shapes=scratch,
        compiler_params=params(16),
    )(columns, lost, split, *operands_vmem)


def eliminate(matrix, target):
    size = matrix.shape[0]
    rows = lax.broadcasted_iota(jnp.int32, target.shape, 0)
    columns = [jnp.broadcast_to(matrix[:, k : k + 1], target.shape) for k in range(size)]
    for k in range(size):
        pivot = columns[k]
        inverse = 1.0 / pivot[k : k + 1, :]
        scaled = pivot * inverse
        here = rows == k
        top = target[k : k + 1, :]
        target = jnp.where(here, top * inverse, target - scaled * top)
        for i in range(k + 1, size):
            entry = pivot[i : i + 1, :]
            columns[i] = jnp.where(here, entry * inverse, columns[i] - scaled * entry)
    return target


def coefficients(gathered, cols):
    g00, g01, g01_t, g02, g02_t, g11, g12 = unpack_gram(jnp.sum(gathered[...], axis=0), cols)
    whole, cross = 0.5 * (g01 + g01_t), 0.5 * (g02 + g11)
    cross_t = 0.5 * (g02_t + g11)
    big = jnp.concatenate(
        [jnp.concatenate([whole, cross], axis=1), jnp.concatenate([cross_t, g12], axis=1)], axis=0
    )
    rows, columns = grid16(cols)
    unit = (rows == columns).astype(jnp.float32)
    advance = eliminate(whole, g00)
    inverse = eliminate(g00, unit)
    moved = dot_nn(jnp.concatenate([g01, g11], axis=0), advance)
    squares = g00 - moved[:cols] - dot_tn(advance, g01_t - moved[cols:])
    mixing = dot_nn(inverse, squares)
    heading = jnp.concatenate([unit + mixing, -advance], axis=0)
    curvature = dot_tn(heading, dot_nn(big, heading))
    second = eliminate(curvature, squares)
    combo = dot_nn(heading, second)
    return jnp.concatenate([combo[:cols] + advance, combo[cols:]], axis=0)


def outer_kernel(
    lost_ref, gathered, right, image, parts_b, parts_y, precond, solution, target, head, kept
):
    blocks, cols, tb = right.shape
    mine = Place(lost_ref).mine
    weights = coefficients(gathered, cols)

    def basis(pick):
        return jnp.concatenate(
            [
                jnp.concatenate([pick(0, i) for i in range(blocks)], axis=1),
                jnp.concatenate([pick(1, i) for i in range(blocks)], axis=1),
            ],
            axis=0,
        )

    parts = (parts_b, parts_y)
    own = (right, image)
    stacked = jnp.concatenate(
        [
            basis(lambda n, i: own[n][i]),
            basis(lambda n, i: parts[n][1, i] + parts[n][2, i]),
            basis(lambda n, i: parts[n][0, i] * (1.0 - mine) + parts[n][2, i]),
        ],
        axis=1,
    )
    made = dot_tn(weights, stacked)
    span = blocks * tb
    for i in range(blocks):
        solution[i] = made[:, i * tb : (i + 1) * tb]
        aim = right[i] - made[:, span + i * tb : span + (i + 1) * tb]
        target[i] = aim
        head[i] = smoothed(aim, precond[i], cols, tb)
        kept[i] = made[:, 2 * span + i * tb : 2 * span + (i + 1) * tb]


def inner_kernel(
    lost_ref, gathered, right, solution, kept, head, smooth, lost0, lost1, recovered, residual
):
    blocks, cols, tb = right.shape
    mine = Place(lost_ref).mine
    weights = coefficients(gathered, cols)
    stacked = jnp.concatenate(
        [
            jnp.concatenate([lanes(head), lanes(lost0)], axis=1),
            jnp.concatenate([lanes(smooth), lanes(lost1)], axis=1),
        ],
        axis=0,
    )
    made = dot_tn(weights, stacked)
    span = blocks * tb
    for i in range(blocks):
        estimate = made[:, i * tb : (i + 1) * tb]
        recovered[i] = jnp.where(mine > 0.5, estimate, solution[i])
        residual[i] = right[i] - kept[i] - made[:, span + i * tb : span + (i + 1) * tb]


def small_call(kernel, outs, lost, gathered, *arrays):
    return pl.pallas_call(
        kernel,
        out_shape=outs,
        in_specs=[spec(SMEM)] + [spec(VMEM)] * (1 + len(arrays)),
        out_specs=[spec(VMEM)] * len(outs),
        compiler_params=params(16),
    )(lost, gathered, *arrays)


def move(value, where, inside=False):
    rows = lax.axis_size("row")
    total = rows * lax.axis_size("grp")
    pairs = [(i, where(i)) for i in range(total) if 0 <= where(i) < total]
    if inside:
        pairs = [(i, j) for i, j in pairs if i // rows == j // rows]
    return lax.ppermute(value, AXES, pairs)


def window(value, inside=False, along=()):
    swapped = move(value, lambda i: i ^ 1)
    pair = jnp.concatenate([value, swapped, *along], axis=0)
    alone = jnp.concatenate([value, along[0]], axis=0) if along else value
    near = move(pair, lambda i: i - 1 if i % 2 == 0 else i + 1, inside)
    far = move(alone, lambda i: i - 3 if i % 2 == 0 else i + 3, inside)
    other = move(near, lambda i: i ^ 1)
    return value, swapped, near, other, far


def exchange(gram):
    return lax.all_to_all(gram, AXES, 0, 0)


def per_device(matrix_tiles, column_index, precond, right_side, lost_group):
    blocks, cols, tb = right_side.shape
    assert -(-BAND // blocks) == REACH <= lax.axis_size("row")
    total = lax.axis_size("row") * lax.axis_size("grp")

    vec = jax.ShapeDtypeStruct(right_side.shape, jnp.float32)
    vec3 = jax.ShapeDtypeStruct((3,) + right_side.shape, jnp.float32)
    gram = jax.ShapeDtypeStruct((total, cols // 2, 8 * cols), jnp.float32)
    assert tb == 8 * cols
    held = VMEM(right_side.shape, jnp.float32)

    split, halves = split_call(matrix_tiles, precond)
    parts_b, image = tile_call(
        first_kernel, 3, [vec3, vec], [], split, window(right_side), column_index, lost_group
    )
    parts_y, gram_outer = tile_call(
        second_kernel, 3, [vec3, gram], [held], split,
        (right_side,) + window(image), column_index, lost_group,
    )
    solution, target, head, kept = small_call(
        outer_kernel, [vec] * 4, lost_group, exchange(gram_outer), right_side, image, parts_b, parts_y, halves
    )
    ahead = window(head, inside=True)
    applied, smooth = tile_call(
        third_kernel, 1, [vec] * 2, [], split, (halves,) + ahead, column_index, lost_group
    )
    lost0, lost1, gram_inner = tile_call(
        fourth_kernel, 3, [vec, vec, gram], [held], split,
        (target, head, applied) + window(smooth, along=ahead[:2]), column_index, lost_group,
    )
    recovered, residual = small_call(
        inner_kernel, [vec] * 2, lost_group, exchange(gram_inner), right_side, solution, kept, head, smooth,
        lost0, lost1,
    )
    return (recovered, residual)


def solution(mesh):
    in_specs = (
        P(("grp", "row"), None, None, None),
        P(("grp", "row"), None),
        P(("grp", "row"), None, None),
        P(("grp", "row"), None, None),
        P(),
    )
    out_specs = (P(("grp", "row"), None, None), P(("grp", "row"), None, None))

    return jax.shard_map(
        per_device, mesh=mesh, in_specs=in_specs, out_specs=out_specs, check_vma=False
    )
```

```python
import jax
import jax.numpy as jnp
from jax import lax
from jax.experimental import pallas as pl
from jax.experimental.pallas import tpu as pltpu
from jax.sharding import PartitionSpec as P


BAND = 12
OFFSETS = (0, 1, -1, -2, 2, 3, -3)
REACH = 3
OWN, LOST, ELSE = range(3)
SLOTS = len(OFFSETS)
STAY = 1
HIGHEST = lax.Precision.HIGHEST
AXES = ("grp", "row")
VMEM = pltpu.VMEM
SMEM = pltpu.SMEM


def spec(space):
    return pl.BlockSpec(memory_space=space)


def params(mib):
    return pltpu.CompilerParams(vmem_limit_bytes=mib << 20)


def dot_nt(former, latter):
    return lax.dot_general(
        former, latter, (((1,), (1,)), ((), ())), precision=HIGHEST,
        preferred_element_type=jnp.float32,
    )


def dot_tn(former, latter):
    return lax.dot_general(
        former, latter, (((0,), (0,)), ((), ())), precision=HIGHEST,
        preferred_element_type=jnp.float32,
    )


def dot_nn(former, latter):
    return jnp.dot(former, latter, precision=HIGHEST, preferred_element_type=jnp.float32)


def split3(value):
    high = value.astype(jnp.bfloat16)
    rest = value - high.astype(jnp.float32)
    middle = rest.astype(jnp.bfloat16)
    low = (rest - middle.astype(jnp.float32)).astype(jnp.bfloat16)
    return high, middle, low


def build_table(pieces, vector, place, table_ref, classes, blocks, cols, start=0):
    v, sw, near, other, far = pieces
    first = vector * blocks
    pair = first + v.shape[0]
    slots = ((v, first), (sw, first), (near, first), (near, pair), (other, first), (other, pair), (far, first))
    for slot, (piece, base) in enumerate(slots):
        position, flags = place.slot(slot)
        for block in range(blocks):
            value = piece[base + block]
            for k, name in enumerate(classes):
                for s, term in enumerate(split3(value * flags[name])):
                    rows = pl.ds((3 * (start + k) + s) * cols, cols)
                    table_ref[position * blocks + block, rows, :] = term


class Joined:
    def __init__(self, first, second):
        self.parts = (first, second)
        self.first = first.shape[0]
        self.shape = (first.shape[0] + second.shape[0], *first.shape[1:])

    def at(self, row):
        return self.parts[row >= self.first].at[row - self.first * (row >= self.first)]


class Place:
    def __init__(self, lost_ref):
        self.me = lax.axis_index(AXES)
        self.row = lax.axis_index("row")
        self.group = lax.axis_index("grp")
        self.rows = lax.axis_size("row")
        self.lost = lax.rem(lost_ref[0], lax.axis_size("grp"))
        self.sign = 1 - 2 * lax.rem(self.me, 2)
        self.mine = jnp.where(self.group == self.lost, 1.0, 0.0)

    def slot(self, slot):
        offset = self.sign * OFFSETS[slot]
        row = self.row + offset
        side = jnp.where(row < 0, -1, jnp.where(row >= self.rows, 1, 0))
        own = jnp.where(side == 0, 1.0, 0.0)
        lost = jnp.where((side != 0) & (self.group + side == self.lost), 1.0, 0.0)
        return offset + REACH, (own, lost, 1.0 - own - lost)

    def base(self, blocks):
        return (self.me - REACH) * blocks


def row_product(columns_ref, base, table_ref, split_ref, row, classes, cols):
    pairs, tb = split_ref.shape[1], split_ref.shape[2] // 2
    total = None
    for pair in range(pairs):
        left = jnp.concatenate(
            [table_ref[columns_ref[row, 2 * pair + j] - base] for j in (0, 1)], axis=1
        )
        part = lax.dot_general(
            left, split_ref.at(row)[pair], (((1,), (0,)), ((), ())),
            preferred_element_type=jnp.float32,
        )
        total = part if total is None else total + part
    total = total[:, :tb] + total[:, tb:]
    out = []
    for k in range(classes):
        base = 3 * k * cols
        out.append(
            total[base : base + cols]
            + total[base + cols : base + 2 * cols]
            + total[base + 2 * cols : base + 3 * cols]
        )
    return out


def split_kernel(
    tiles_hbm, precond_hbm, right_hbm, split_a, split_b, halves, smooth, tiles, precond, right, sems, late_sems
):
    blocks, count, tb, _ = tiles.shape
    rows, columns = grid16(2 * tb)
    unit = (rows == columns).astype(jnp.bfloat16)
    copies = [
        pltpu.make_async_copy(tiles_hbm.at[row], tiles.at[row], sems.at[row])
        for row in range(blocks)
    ]
    for copy in copies:
        copy.start()
    late = [
        pltpu.make_async_copy(precond_hbm, precond, late_sems.at[0]),
        pltpu.make_async_copy(right_hbm, right, late_sems.at[1]),
    ]
    for copy in late:
        copy.start()
    for row in range(blocks):
        copies[row].wait()
        for pair in range(count // 2):
            highs, rests = [], []
            for k in (2 * pair, 2 * pair + 1):
                tile = tiles[row, k]
                high = tile.astype(jnp.bfloat16)
                highs.append(high)
                rests.append((tile - high.astype(jnp.float32)).astype(jnp.bfloat16))
            both = jnp.concatenate(
                [jnp.concatenate(highs, axis=1), jnp.concatenate(rests, axis=1)], axis=0
            )
            turned = lax.dot_general(
                unit, both, (((1,), (1,)), ((), ())), preferred_element_type=jnp.float32
            )
            Joined(split_a, split_b).at(row)[pair] = turned.astype(jnp.bfloat16)
    for copy in late:
        copy.wait()
    for row in range(blocks):
        high = precond[row].astype(jnp.bfloat16)
        halves[row, 0:tb] = high
        halves[row, tb : 2 * tb] = (precond[row] - high.astype(jnp.float32)).astype(jnp.bfloat16)
    for row in range(blocks):
        smooth[row] = smoothed(right[row], halves[row], right.shape[1], tb)


def split_call(tiles, precond, right):
    blocks, count, tb, _ = tiles.shape
    return pl.pallas_call(
        split_kernel,
        out_shape=[
            jax.ShapeDtypeStruct((rows, count // 2, 2 * tb, 2 * tb), jnp.bfloat16)
            for rows in (STAY, blocks - STAY)
        ]
        + [
            jax.ShapeDtypeStruct((blocks, 2 * tb, tb), jnp.bfloat16),
            jax.ShapeDtypeStruct(right.shape, jnp.float32),
        ],
        in_specs=[spec(pltpu.HBM)] * 3,
        out_specs=[spec(VMEM)] * 4,
        scratch_shapes=[
            VMEM(tiles.shape, jnp.float32),
            VMEM(precond.shape, jnp.float32),
            VMEM(right.shape, jnp.float32),
            pltpu.SemaphoreType.DMA((blocks,)),
            pltpu.SemaphoreType.DMA((2,)),
        ],
        compiler_params=params(24),
        cost_estimate=pl.CostEstimate(flops=0, bytes_accessed=12 * tiles.size // 2, transcendentals=0),
    )(*(pltpu.with_memory_space_constraint(array, pltpu.HBM) for array in (tiles, precond, right)))


def smoothed(value, halves, cols, tb):
    left = jnp.concatenate(split3(value), axis=0)
    both = lax.dot_general(
        left, halves, (((1,), (1,)), ((), ())), preferred_element_type=jnp.float32
    )
    both = both[:, :tb] + both[:, tb:]
    return both[:cols] + both[cols : 2 * cols] + both[2 * cols :]


def lanes(ref):
    return jnp.concatenate([ref[i] for i in range(ref.shape[0])], axis=1)


def grid16(cols):
    rows = lax.broadcasted_iota(jnp.int32, (cols, cols), 0)
    columns = lax.broadcasted_iota(jnp.int32, (cols, cols), 1)
    return rows, columns


def pack_gram(gram_ref, former, latter, scale, cols):
    gram = dot_nt(former, latter)
    if scale is not None:
        gram = gram * scale
    g00, g01, g02 = (gram[:cols, k * cols : (k + 1) * cols] for k in range(3))
    g11, g12 = (gram[cols:, k * cols : (k + 1) * cols] for k in (1, 2))
    rows, columns = grid16(cols)
    upper = rows <= columns
    first = jnp.where(upper, g00, g11)
    middle = jnp.sum(jnp.where(rows == columns, g11, 0.0), axis=1, keepdims=True)
    last = jnp.where(rows == columns + 1, middle, 0.0)
    last = jnp.where((rows == cols - 1) & (columns == 0), g11[0:1, 0:1], last)
    last = jnp.where(upper, 0.5 * (g12 + g12.T), last)
    flat = jnp.concatenate([first, g01, g02, last], axis=1)
    half = cols // 2
    packed = jnp.concatenate([flat[:half], flat[half:]], axis=1)
    gram_ref[...] = jnp.broadcast_to(packed[None], gram_ref.shape)


def unpack_gram(packed, cols):
    width = packed.shape[1] // 2
    flat = jnp.concatenate([packed[:, :width], packed[:, width:]], axis=0)
    turned = flat.T
    first, g01, g02, last = (flat[:, k * cols : (k + 1) * cols] for k in range(4))
    first_t, g01_t, g02_t, last_t = (turned[k * cols : (k + 1) * cols] for k in range(4))
    rows, columns = grid16(cols)
    upper = rows <= columns
    g00 = jnp.where(upper, first, first_t)
    middle = jnp.sum(jnp.where(rows == columns + 1, last, 0.0), axis=1, keepdims=True)
    middle = jnp.where(rows == 0, last[cols - 1 : cols, 0:1], middle)
    g11 = jnp.where(rows > columns, first, jnp.where(rows < columns, first_t, middle))
    g12 = jnp.where(upper, last, last_t)
    return g00, g01, g01_t, g02, g02_t, g11, g12


def first_kernel(
    columns_ref, lost_ref, split_a, split_b, halves, v, sw, p1, p2, p3, parts, image, smooth, table
):
    blocks, cols, _ = v.shape
    place = Place(lost_ref)
    base = place.base(blocks)
    build_table((v, sw, p1, p2, p3), 0, place, table, (OWN, LOST, ELSE), blocks, cols)
    for row in range(blocks):
        out = row_product(columns_ref, base, table, Joined(split_a, split_b), row, 3, cols)
        for k in range(3):
            parts[k, row] = out[k]
        image[row] = out[0] + out[1] + out[2]
    for row in range(blocks):
        smooth[row] = smoothed(parts[1, row] + parts[2, row], halves[row], cols, v.shape[2])


def second_kernel(
    columns_ref, lost_ref, split_a, split_b, halves, smooth_b, smooth_o, right, v, sw, p1, p2, p3,
    parts, gram, smooth, table, image,
):
    blocks, cols, _ = v.shape
    place = Place(lost_ref)
    base = place.base(blocks)
    build_table((v, sw, p1, p2, p3), 0, place, table, (OWN, LOST, ELSE), blocks, cols)
    for row in range(blocks):
        out = row_product(columns_ref, base, table, Joined(split_a, split_b), row, 3, cols)
        for k in range(3):
            parts[k, row] = out[k]
        image[row] = out[0] + out[1] + out[2]
    for row in range(blocks):
        smooth[row] = smooth_b[row]
        smooth[blocks + row] = smooth_o[row]
        smooth[2 * blocks + row] = smoothed(
            parts[1, row] + parts[2, row], halves[row], cols, v.shape[2]
        )
    former = jnp.concatenate([lanes(right), lanes(v)], axis=0)
    latter = jnp.concatenate([former, lanes(image)], axis=0)
    pack_gram(gram, former, latter, None, cols)


def third_kernel(
    columns_ref, lost_ref, split_a, split_hbm, v, sw, p1, p2, p3, applied, table, split_b, sems
):
    blocks, cols = applied.shape[1], v.shape[1]
    copies = [
        pltpu.make_async_copy(split_hbm.at[row], split_b.at[row], sems.at[row])
        for row in range(blocks - STAY)
    ]
    for copy in copies:
        copy.start()
    place = Place(lost_ref)
    base = place.base(blocks)
    for vector in range(3):
        build_table((v, sw, p1, p2, p3), vector, place, table, (OWN,), blocks, cols, vector)
    for row in range(blocks):
        if row >= STAY:
            copies[row - STAY].wait()
        out = row_product(columns_ref, base, table, Joined(split_a, split_b), row, 3, cols)
        for vector in range(3):
            applied[vector, row] = out[vector]


def fourth_kernel(
    columns_ref, lost_ref, split_a, split_b, target, applied, v, sw, p1, p2, p3, lost0, lost1, gram,
    table, second,
):
    blocks, cols, _ = target.shape
    place = Place(lost_ref)
    base = place.base(blocks)
    mine = place.mine
    build_table((v, sw, p1, p2, p3), 0, place, table, (OWN, LOST), blocks, cols)
    build_table((v, sw, p1, p2, p3), 1, place, table, (LOST,), blocks, cols, 2)
    for row in range(blocks):
        out = row_product(columns_ref, base, table, Joined(split_a, split_b), row, 3, cols)
        second[row] = out[0]
        lost1[row] = out[0] * mine + out[1]
        lost0[row] = applied[row] * mine + out[2]
    smooth, head = v.at[0:blocks], v.at[blocks : 2 * blocks]
    former = jnp.concatenate([lanes(head), lanes(smooth)], axis=0)
    latter = jnp.concatenate([lanes(target), lanes(applied), lanes(second)], axis=0)
    pack_gram(gram, former, latter, mine, cols)


def tile_call(kernel, classes, outs, extra, split, operands_vmem, columns, lost, place=VMEM):
    blocks = split[0].shape[0] + split[1].shape[0]
    _, cols, tb = operands_vmem[-1].shape
    scratch = [VMEM((SLOTS * blocks, 3 * classes * cols, tb), jnp.bfloat16)] + extra
    return pl.pallas_call(
        kernel,
        out_shape=outs,
        in_specs=[spec(SMEM), spec(SMEM), spec(VMEM), spec(place)]
        + [spec(VMEM)] * len(operands_vmem),
        out_specs=[spec(VMEM)] * len(outs),
        scratch_shapes=scratch,
        compiler_params=params(16),
    )(columns, lost, *split, *operands_vmem)


def eliminate(matrix, target):
    size = matrix.shape[0]
    rows = lax.broadcasted_iota(jnp.int32, target.shape, 0)
    columns = [jnp.broadcast_to(matrix[:, k : k + 1], target.shape) for k in range(size)]
    for k in range(size):
        pivot = columns[k]
        inverse = 1.0 / pivot[k : k + 1, :]
        scaled = pivot * inverse
        here = rows == k
        top = target[k : k + 1, :]
        target = jnp.where(here, top * inverse, target - scaled * top)
        for i in range(k + 1, size):
            entry = pivot[i : i + 1, :]
            columns[i] = jnp.where(here, entry * inverse, columns[i] - scaled * entry)
    return target


def coefficients(gathered, cols):
    g00, g01, g01_t, g02, g02_t, g11, g12 = unpack_gram(jnp.sum(gathered[...], axis=0), cols)
    whole, cross = 0.5 * (g01 + g01_t), 0.5 * (g02 + g11)
    cross_t = 0.5 * (g02_t + g11)
    big = jnp.concatenate(
        [jnp.concatenate([whole, cross], axis=1), jnp.concatenate([cross_t, g12], axis=1)], axis=0
    )
    rows, columns = grid16(cols)
    unit = (rows == columns).astype(jnp.float32)
    advance = eliminate(whole, g00)
    inverse = eliminate(g00, unit)
    moved = dot_nn(jnp.concatenate([g01, g11], axis=0), advance)
    squares = g00 - moved[:cols] - dot_tn(advance, g01_t - moved[cols:])
    mixing = dot_nn(inverse, squares)
    heading = jnp.concatenate([unit + mixing, -advance], axis=0)
    curvature = dot_tn(heading, dot_nn(big, heading))
    second = eliminate(curvature, squares)
    combo = dot_nn(heading, second)
    return jnp.concatenate([combo[:cols] + advance, combo[cols:]], axis=0)


def outer_kernel(
    lost_ref, gathered, right, image, parts_b, parts_y, smooth, moved, halves,
    solution, target, applied, kept, pair,
):
    blocks, cols, tb = right.shape
    mine = Place(lost_ref).mine
    weights = coefficients(gathered, cols)
    span = blocks * tb

    def wide(pick):
        return jnp.concatenate([pick(i) for i in range(blocks)], axis=1)

    def others(parts):
        return wide(lambda i: parts[1, i] + parts[2, i])

    def kept_part(parts):
        return wide(lambda i: parts[0, i] * (1.0 - mine) + parts[2, i])

    stacked = jnp.concatenate(
        [
            jnp.concatenate([lanes(right), lanes(image)], axis=0),
            jnp.concatenate([kept_part(parts_b), kept_part(parts_y)], axis=0),
            jnp.concatenate([others(parts_b), others(parts_y)], axis=0),
            jnp.concatenate(
                [wide(lambda i: smooth[blocks + i]), wide(lambda i: smooth[2 * blocks + i])], axis=0
            ),
            jnp.concatenate([wide(lambda i: moved[1, i]), wide(lambda i: moved[2, i])], axis=0),
        ],
        axis=1,
    )
    made = dot_tn(weights, stacked)

    def block(number, i):
        return made[:, number * span + i * tb : number * span + (i + 1) * tb]

    for i in range(blocks):
        solution[i] = block(0, i)
        kept[i] = block(1, i)
        target[i] = right[i] - block(2, i)
        pair[blocks + i] = smooth[i] - block(3, i)
        image_of_head = moved[0, i] - block(4, i)
        applied[i] = image_of_head
        pair[i] = smoothed(image_of_head, halves[i], cols, tb)


def inner_kernel(
    lost_ref, gathered, right, solution, kept, pair, lost0, lost1, recovered, residual
):
    blocks, cols, tb = right.shape
    mine = Place(lost_ref).mine
    weights = coefficients(gathered, cols)
    smooth, head = pair.at[0:blocks], pair.at[blocks : 2 * blocks]
    stacked = jnp.concatenate(
        [
            jnp.concatenate([lanes(head), lanes(lost0)], axis=1),
            jnp.concatenate([lanes(smooth), lanes(lost1)], axis=1),
        ],
        axis=0,
    )
    made = dot_tn(weights, stacked)
    span = blocks * tb
    for i in range(blocks):
        estimate = made[:, i * tb : (i + 1) * tb]
        recovered[i] = jnp.where(mine > 0.5, estimate, solution[i])
        residual[i] = right[i] - kept[i] - made[:, span + i * tb : span + (i + 1) * tb]


def reload_kernel(split_hbm, split, sems):
    blocks, pairs = split.shape[0], split.shape[1]
    chunk = pairs // 4
    copies = [
        pltpu.make_async_copy(
            split_hbm.at[row, k * chunk : (k + 1) * chunk],
            split.at[row, k * chunk : (k + 1) * chunk],
            sems.at[row, k],
        )
        for row in range(blocks)
        for k in range(4)
    ]
    for copy in copies:
        copy.start()
    for copy in copies:
        copy.wait()


def reload_call(split):
    return pl.pallas_call(
        reload_kernel,
        out_shape=jax.ShapeDtypeStruct(split.shape, split.dtype),
        in_specs=[spec(pltpu.HBM)],
        out_specs=spec(VMEM),
        scratch_shapes=[pltpu.SemaphoreType.DMA((split.shape[0], 4))],
        compiler_params=params(16),
        cost_estimate=pl.CostEstimate(flops=0, bytes_accessed=4 * split.size, transcendentals=0),
    )(split)


def small_call(kernel, outs, lost, gathered, *arrays):
    return pl.pallas_call(
        kernel,
        out_shape=outs,
        in_specs=[spec(SMEM)] + [spec(VMEM)] * (1 + len(arrays)),
        out_specs=[spec(VMEM)] * len(outs),
        compiler_params=params(16),
    )(lost, gathered, *arrays)


def move(value, where, inside=False):
    rows = lax.axis_size("row")
    total = rows * lax.axis_size("grp")
    pairs = [(i, where(i)) for i in range(total) if 0 <= where(i) < total]
    if inside:
        pairs = [(i, j) for i, j in pairs if i // rows == j // rows]
    return lax.ppermute(value, AXES, pairs)


def window(value, inside=False):
    swapped = move(value, lambda i: i ^ 1)
    pair = jnp.concatenate([value, swapped], axis=0)
    near = move(pair, lambda i: i - 1 if i % 2 == 0 else i + 1, inside)
    far = move(value, lambda i: i - 3 if i % 2 == 0 else i + 3, inside)
    other = move(near, lambda i: i ^ 1)
    return value, swapped, near, other, far


def exchange(gram):
    return lax.all_to_all(gram, AXES, 0, 0)


def per_device(matrix_tiles, column_index, precond, right_side, lost_group):
    blocks, cols, tb = right_side.shape
    assert -(-BAND // blocks) == REACH <= lax.axis_size("row")
    total = lax.axis_size("row") * lax.axis_size("grp")

    def shape(*lead):
        return jax.ShapeDtypeStruct((*lead, cols, tb), jnp.float32)

    vec, vec3 = shape(blocks), shape(3, blocks)
    gram = jax.ShapeDtypeStruct((total, cols // 2, 8 * cols), jnp.float32)
    assert tb == 8 * cols
    held = VMEM(right_side.shape, jnp.float32)
    placing = (column_index, lost_group)

    *split, halves, smooth_b = split_call(matrix_tiles, precond, right_side)
    parts_b, image, smooth_o = tile_call(
        first_kernel, 3, [vec3, vec, vec], [], split,
        (halves,) + window(right_side), *placing,
    )
    parts_y, gram_outer, smooth = tile_call(
        second_kernel, 3, [vec3, gram, shape(3 * blocks)], [held], split,
        (halves, smooth_b, smooth_o, right_side) + window(image), *placing,
    )
    around = window(smooth, inside=True)
    gathered = exchange(gram_outer)
    held_split = pltpu.with_memory_space_constraint(split[1], pltpu.HBM)
    (moved,) = tile_call(
        third_kernel, 3, [vec3],
        [VMEM(split[1].shape, split[1].dtype), pltpu.SemaphoreType.DMA((blocks - STAY,))],
        (split[0], held_split), around, *placing, place=pltpu.HBM,
    )
    solution, target, applied, kept, pair = small_call(
        outer_kernel, [vec] * 4 + [shape(2 * blocks)], lost_group, gathered, right_side, image,
        parts_b, parts_y, smooth, moved, halves,
    )
    split = (split[0], reload_call(held_split))
    lost0, lost1, gram_inner = tile_call(
        fourth_kernel, 3, [vec, vec, gram], [held], split,
        (target, applied) + window(pair), *placing,
    )
    recovered, residual = small_call(
        inner_kernel, [vec] * 2, lost_group, exchange(gram_inner), right_side, solution, kept, pair,
        lost0, lost1,
    )
    return (recovered, residual)


def solution(mesh):
    in_specs = (
        P(("grp", "row"), None, None, None),
        P(("grp", "row"), None),
        P(("grp", "row"), None, None),
        P(("grp", "row"), None, None),
        P(),
    )
    out_specs = (P(("grp", "row"), None, None), P(("grp", "row"), None, None))

    return jax.shard_map(
        per_device, mesh=mesh, in_specs=in_specs, out_specs=out_specs, check_vma=False
    )
```

```python
import jax
import jax.numpy as jnp
from jax import lax
from jax.experimental import pallas as pl
from jax.experimental.pallas import tpu as pltpu
from jax.sharding import PartitionSpec as P


BAND = 12
OFFSETS = (0, 1, -1, -2, 2, 3, -3)
REACH = 3
OWN, LOST, ELSE = range(3)
SLOTS = len(OFFSETS)
TERMS = 2
STAY = 1
HIGHEST = lax.Precision.HIGHEST
AXES = ("grp", "row")
VMEM = pltpu.VMEM
SMEM = pltpu.SMEM


def spec(space):
    return pl.BlockSpec(memory_space=space)


def params(mib):
    return pltpu.CompilerParams(vmem_limit_bytes=mib << 20)


def dot_nt(former, latter):
    return lax.dot_general(
        former, latter, (((1,), (1,)), ((), ())), precision=HIGHEST,
        preferred_element_type=jnp.float32,
    )


def dot_tn(former, latter):
    return lax.dot_general(
        former, latter, (((0,), (0,)), ((), ())), precision=HIGHEST,
        preferred_element_type=jnp.float32,
    )


def dot_nn(former, latter):
    return jnp.dot(former, latter, precision=HIGHEST, preferred_element_type=jnp.float32)


def terms_of(value):
    high = value.astype(jnp.bfloat16)
    return high, (value - high.astype(jnp.float32)).astype(jnp.bfloat16)


def build_table(pieces, vector, place, table_ref, classes, blocks, cols, start=0):
    v, sw, near, other, far = pieces
    first = vector * blocks
    pair = first + v.shape[0]
    slots = ((v, first), (sw, first), (near, first), (near, pair), (other, first), (other, pair), (far, first))
    for slot, (piece, base) in enumerate(slots):
        position, flags = place.slot(slot)
        for block in range(blocks):
            value = piece[base + block]
            for k, name in enumerate(classes):
                for s, term in enumerate(terms_of(value * flags[name])):
                    rows = pl.ds((TERMS * (start + k) + s) * cols, cols)
                    table_ref[position * blocks + block, rows, :] = term


class Joined:
    def __init__(self, first, second):
        self.parts = (first, second)
        self.first = first.shape[0]
        self.shape = (first.shape[0] + second.shape[0], *first.shape[1:])

    def at(self, row):
        return self.parts[row >= self.first].at[row - self.first * (row >= self.first)]


class Place:
    def __init__(self, lost_ref):
        self.me = lax.axis_index(AXES)
        self.row = lax.axis_index("row")
        self.group = lax.axis_index("grp")
        self.rows = lax.axis_size("row")
        self.lost = lax.rem(lost_ref[0], lax.axis_size("grp"))
        self.sign = 1 - 2 * lax.rem(self.me, 2)
        self.mine = jnp.where(self.group == self.lost, 1.0, 0.0)

    def slot(self, slot):
        offset = self.sign * OFFSETS[slot]
        row = self.row + offset
        side = jnp.where(row < 0, -1, jnp.where(row >= self.rows, 1, 0))
        own = jnp.where(side == 0, 1.0, 0.0)
        lost = jnp.where((side != 0) & (self.group + side == self.lost), 1.0, 0.0)
        return offset + REACH, (own, lost, 1.0 - own - lost)

    def base(self, blocks):
        return (self.me - REACH) * blocks


def row_product(columns_ref, base, table_ref, split_ref, row, classes, cols):
    pairs, tb = split_ref.shape[1], split_ref.shape[2] // 2
    total = None
    for pair in range(pairs):
        left = jnp.concatenate(
            [table_ref[columns_ref[row, 2 * pair + j] - base] for j in (0, 1)], axis=1
        )
        part = lax.dot_general(
            left, split_ref.at(row)[pair], (((1,), (0,)), ((), ())),
            preferred_element_type=jnp.float32,
        )
        total = part if total is None else total + part
    total = total[:, :tb] + total[:, tb:]
    out = []
    for k in range(classes):
        base = TERMS * k * cols
        out.append(total[base : base + cols] + total[base + cols : base + 2 * cols])
    return out


def split_kernel(
    tiles_hbm, precond_hbm, right_hbm, split_a, split_b, halves, smooth, tiles, precond, right, sems, late_sems
):
    blocks, count, tb, _ = tiles.shape
    rows, columns = grid16(2 * tb)
    unit = (rows == columns).astype(jnp.bfloat16)
    copies = [
        pltpu.make_async_copy(tiles_hbm.at[row], tiles.at[row], sems.at[row])
        for row in range(blocks)
    ]
    for copy in copies:
        copy.start()
    late = [
        pltpu.make_async_copy(precond_hbm, precond, late_sems.at[0]),
        pltpu.make_async_copy(right_hbm, right, late_sems.at[1]),
    ]
    for copy in late:
        copy.start()
    for row in range(blocks):
        copies[row].wait()
        for pair in range(count // 2):
            place = Joined(split_a, split_b).at(row)
            if pair % 2 == 1:
                for k in (0, 1):
                    tile = tiles[row, 2 * pair + k].T
                    high = tile.astype(jnp.bfloat16)
                    place[pair, k * tb : (k + 1) * tb, 0:tb] = high
                    place[pair, k * tb : (k + 1) * tb, tb : 2 * tb] = (
                        tile - high.astype(jnp.float32)
                    ).astype(jnp.bfloat16)
                continue
            highs, rests = [], []
            for k in (2 * pair, 2 * pair + 1):
                tile = tiles[row, k]
                high = tile.astype(jnp.bfloat16)
                highs.append(high)
                rests.append((tile - high.astype(jnp.float32)).astype(jnp.bfloat16))
            both = jnp.concatenate(
                [jnp.concatenate(highs, axis=1), jnp.concatenate(rests, axis=1)], axis=0
            )
            turned = lax.dot_general(
                unit, both, (((1,), (1,)), ((), ())), preferred_element_type=jnp.float32
            )
            place[pair] = turned.astype(jnp.bfloat16)
    for copy in late:
        copy.wait()
    for row in range(blocks):
        high = precond[row].astype(jnp.bfloat16)
        halves[row, 0:tb] = high
        halves[row, tb : 2 * tb] = (precond[row] - high.astype(jnp.float32)).astype(jnp.bfloat16)
    for row in range(blocks):
        smooth[row] = smoothed(right[row], halves[row], right.shape[1], tb)


def split_call(tiles, precond, right):
    blocks, count, tb, _ = tiles.shape
    return pl.pallas_call(
        split_kernel,
        out_shape=[
            jax.ShapeDtypeStruct((rows, count // 2, 2 * tb, 2 * tb), jnp.bfloat16)
            for rows in (STAY, blocks - STAY)
        ]
        + [
            jax.ShapeDtypeStruct((blocks, 2 * tb, tb), jnp.bfloat16),
            jax.ShapeDtypeStruct(right.shape, jnp.float32),
        ],
        in_specs=[spec(pltpu.HBM)] * 3,
        out_specs=[spec(VMEM)] * 4,
        scratch_shapes=[
            VMEM(tiles.shape, jnp.float32),
            VMEM(precond.shape, jnp.float32),
            VMEM(right.shape, jnp.float32),
            pltpu.SemaphoreType.DMA((blocks,)),
            pltpu.SemaphoreType.DMA((2,)),
        ],
        compiler_params=params(24),
        cost_estimate=pl.CostEstimate(flops=0, bytes_accessed=12 * tiles.size // 2, transcendentals=0),
    )(*(pltpu.with_memory_space_constraint(array, pltpu.HBM) for array in (tiles, precond, right)))


def smoothed(value, halves, cols, tb):
    left = jnp.concatenate(terms_of(value), axis=0)
    both = lax.dot_general(
        left, halves, (((1,), (1,)), ((), ())), preferred_element_type=jnp.float32
    )
    both = both[:, :tb] + both[:, tb:]
    return both[:cols] + both[cols:]


def lanes(ref):
    return jnp.concatenate([ref[i] for i in range(ref.shape[0])], axis=1)


def grid16(cols):
    rows = lax.broadcasted_iota(jnp.int32, (cols, cols), 0)
    columns = lax.broadcasted_iota(jnp.int32, (cols, cols), 1)
    return rows, columns


def pack_gram(gram_ref, early, late, turned, scale, cols):
    if scale is not None:
        early, late, turned = early * scale, late * scale, turned * scale
    g00, g01, g11 = early[:cols, :cols], early[:cols, cols:], early[cols:, cols:]
    g02, g12 = late[:cols], late[cols:]
    rows, columns = grid16(cols)
    upper = rows <= columns
    first = jnp.where(upper, g00, g11)
    middle = jnp.sum(jnp.where(rows == columns, g11, 0.0), axis=1, keepdims=True)
    last = jnp.where(rows == columns + 1, middle, 0.0)
    last = jnp.where((rows == cols - 1) & (columns == 0), g11[0:1, 0:1], last)
    last = jnp.where(upper, 0.5 * (g12 + turned), last)
    flat = jnp.concatenate([first, g01, g02, last], axis=1)
    half = cols // 2
    packed = jnp.concatenate([flat[:half], flat[half:]], axis=1)
    gram_ref[...] = jnp.broadcast_to(packed[None], gram_ref.shape)


def unpack_gram(packed, cols):
    width = packed.shape[1] // 2
    flat = jnp.concatenate([packed[:, :width], packed[:, width:]], axis=0)
    turned = flat.T
    first, g01, g02, last = (flat[:, k * cols : (k + 1) * cols] for k in range(4))
    first_t, g01_t, g02_t, last_t = (turned[k * cols : (k + 1) * cols] for k in range(4))
    rows, columns = grid16(cols)
    upper = rows <= columns
    g00 = jnp.where(upper, first, first_t)
    middle = jnp.sum(jnp.where(rows == columns + 1, last, 0.0), axis=1, keepdims=True)
    middle = jnp.where(rows == 0, last[cols - 1 : cols, 0:1], middle)
    g11 = jnp.where(rows > columns, first, jnp.where(rows < columns, first_t, middle))
    g12 = jnp.where(upper, last, last_t)
    return g00, g01, g01_t, g02, g02_t, g11, g12


def first_kernel(
    columns_ref, lost_ref, split_a, split_b, halves, v, sw, p1, p2, p3, parts, image, smooth, table
):
    blocks, cols, _ = v.shape
    place = Place(lost_ref)
    base = place.base(blocks)
    build_table((v, sw, p1, p2, p3), 0, place, table, (OWN, LOST, ELSE), blocks, cols)
    for row in range(blocks):
        out = row_product(columns_ref, base, table, Joined(split_a, split_b), row, 3, cols)
        for k in range(3):
            parts[k, row] = out[k]
        image[row] = out[0] + out[1] + out[2]
    for row in range(blocks):
        smooth[row] = smoothed(parts[1, row] + parts[2, row], halves[row], cols, v.shape[2])


def second_kernel(
    columns_ref, lost_ref, split_a, split_b, halves, smooth_b, smooth_o, right, v, sw, p1, p2, p3,
    parts, gram, smooth, table, image,
):
    blocks, cols, _ = v.shape
    place = Place(lost_ref)
    base = place.base(blocks)
    build_table((v, sw, p1, p2, p3), 0, place, table, (OWN, LOST, ELSE), blocks, cols)
    former = jnp.concatenate([lanes(right), lanes(v)], axis=0)
    early = dot_nt(former, former)
    for row in range(blocks):
        out = row_product(columns_ref, base, table, Joined(split_a, split_b), row, 3, cols)
        for k in range(3):
            parts[k, row] = out[k]
        image[row] = out[0] + out[1] + out[2]
    for row in range(blocks):
        smooth[row] = smooth_b[row]
        smooth[blocks + row] = smooth_o[row]
        smooth[2 * blocks + row] = smoothed(
            parts[1, row] + parts[2, row], halves[row], cols, v.shape[2]
        )
    late = dot_nt(former, lanes(image))
    turned = dot_nt(lanes(image), lanes(v))
    pack_gram(gram, early, late, turned, None, cols)


def third_kernel(
    columns_ref, lost_ref, split_a, split_hbm, v, sw, p1, p2, p3, applied, table, split_b, sems
):
    blocks, cols = applied.shape[1], v.shape[1]
    copies = [
        pltpu.make_async_copy(split_hbm.at[row], split_b.at[row], sems.at[row])
        for row in range(blocks - STAY)
    ]
    for copy in copies:
        copy.start()
    place = Place(lost_ref)
    base = place.base(blocks)
    for vector in range(3):
        build_table((v, sw, p1, p2, p3), vector, place, table, (OWN,), blocks, cols, vector)
    for row in range(blocks):
        if row >= STAY:
            copies[row - STAY].wait()
        out = row_product(columns_ref, base, table, Joined(split_a, split_b), row, 3, cols)
        for vector in range(3):
            applied[vector, row] = out[vector]


def fourth_kernel(
    columns_ref, lost_ref, split_a, split_b, target, applied, v, sw, p1, p2, p3, lost0, lost1, gram,
    table, second,
):
    blocks, cols, _ = target.shape
    place = Place(lost_ref)
    base = place.base(blocks)
    mine = place.mine
    build_table((v, sw, p1, p2, p3), 0, place, table, (OWN, LOST), blocks, cols)
    build_table((v, sw, p1, p2, p3), 1, place, table, (LOST,), blocks, cols, 2)
    smooth, head = v.at[0:blocks], v.at[blocks : 2 * blocks]
    former = jnp.concatenate([lanes(head), lanes(smooth)], axis=0)
    early = dot_nt(former, jnp.concatenate([lanes(target), lanes(applied)], axis=0))
    for row in range(blocks):
        out = row_product(columns_ref, base, table, Joined(split_a, split_b), row, 3, cols)
        second[row] = out[0]
        lost1[row] = out[0] * mine + out[1]
        lost0[row] = applied[row] * mine + out[2]
    late = dot_nt(former, lanes(second))
    turned = dot_nt(lanes(second), lanes(smooth))
    pack_gram(gram, early, late, turned, mine, cols)


def tile_call(kernel, classes, outs, extra, split, operands_vmem, columns, lost, place=VMEM):
    blocks = split[0].shape[0] + split[1].shape[0]
    _, cols, tb = operands_vmem[-1].shape
    scratch = [VMEM((SLOTS * blocks, TERMS * classes * cols, tb), jnp.bfloat16)] + extra
    return pl.pallas_call(
        kernel,
        out_shape=outs,
        in_specs=[spec(SMEM), spec(SMEM), spec(VMEM), spec(place)]
        + [spec(VMEM)] * len(operands_vmem),
        out_specs=[spec(VMEM)] * len(outs),
        scratch_shapes=scratch,
        compiler_params=params(16),
    )(columns, lost, *split, *operands_vmem)


def eliminate(matrix, target):
    size = matrix.shape[0]
    rows = lax.broadcasted_iota(jnp.int32, target.shape, 0)
    columns = [jnp.broadcast_to(matrix[:, k : k + 1], target.shape) for k in range(size)]
    for k in range(size):
        pivot = columns[k]
        inverse = 1.0 / pivot[k : k + 1, :]
        scaled = pivot * inverse
        here = rows == k
        top = target[k : k + 1, :]
        target = jnp.where(here, top * inverse, target - scaled * top)
        for i in range(k + 1, size):
            entry = pivot[i : i + 1, :]
            columns[i] = jnp.where(here, entry * inverse, columns[i] - scaled * entry)
    return target


def coefficients(gathered, cols):
    g00, g01, g01_t, g02, g02_t, g11, g12 = unpack_gram(jnp.sum(gathered[...], axis=0), cols)
    whole, cross = 0.5 * (g01 + g01_t), 0.5 * (g02 + g11)
    cross_t = 0.5 * (g02_t + g11)
    big = jnp.concatenate(
        [jnp.concatenate([whole, cross], axis=1), jnp.concatenate([cross_t, g12], axis=1)], axis=0
    )
    rows, columns = grid16(cols)
    unit = (rows == columns).astype(jnp.float32)
    advance = eliminate(whole, g00)
    inverse = eliminate(g00, unit)
    moved = dot_nn(jnp.concatenate([g01, g11], axis=0), advance)
    squares = g00 - moved[:cols] - dot_tn(advance, g01_t - moved[cols:])
    start = jnp.concatenate([unit, -advance], axis=0)
    mixing = dot_nn(inverse, squares)
    heading = jnp.concatenate([unit + mixing, -advance], axis=0)
    turned = dot_nn(big, start) + dot_nn(dot_nn(big[:, :cols], inverse), squares)
    curvature = dot_tn(heading, turned)
    second = eliminate(curvature, squares)
    combo = dot_nn(heading, second)
    return jnp.concatenate([combo[:cols] + advance, combo[cols:]], axis=0)


def outer_kernel(
    lost_ref, gathered, right, image, parts_b, parts_y, smooth, moved, halves,
    solution, target, applied, kept, pair,
):
    blocks, cols, tb = right.shape
    mine = Place(lost_ref).mine
    weights = coefficients(gathered, cols)
    span = blocks * tb

    def wide(pick):
        return jnp.concatenate([pick(i) for i in range(blocks)], axis=1)

    def others(parts):
        return wide(lambda i: parts[1, i] + parts[2, i])

    def kept_part(parts):
        return wide(lambda i: parts[0, i] * (1.0 - mine) + parts[2, i])

    stacked = jnp.concatenate(
        [
            jnp.concatenate([lanes(right), lanes(image)], axis=0),
            jnp.concatenate([kept_part(parts_b), kept_part(parts_y)], axis=0),
            jnp.concatenate([others(parts_b), others(parts_y)], axis=0),
            jnp.concatenate(
                [wide(lambda i: smooth[blocks + i]), wide(lambda i: smooth[2 * blocks + i])], axis=0
            ),
            jnp.concatenate([wide(lambda i: moved[1, i]), wide(lambda i: moved[2, i])], axis=0),
        ],
        axis=1,
    )
    made = dot_tn(weights, stacked)

    def block(number, i):
        return made[:, number * span + i * tb : number * span + (i + 1) * tb]

    for i in range(blocks):
        solution[i] = block(0, i)
        kept[i] = block(1, i)
        target[i] = right[i] - block(2, i)
        pair[blocks + i] = smooth[i] - block(3, i)
        image_of_head = moved[0, i] - block(4, i)
        applied[i] = image_of_head
        pair[i] = smoothed(image_of_head, halves[i], cols, tb)


def inner_kernel(
    lost_ref, gathered, right, solution, kept, pair, lost0, lost1, recovered, residual
):
    blocks, cols, tb = right.shape
    mine = Place(lost_ref).mine
    weights = coefficients(gathered, cols)
    smooth, head = pair.at[0:blocks], pair.at[blocks : 2 * blocks]
    stacked = jnp.concatenate(
        [
            jnp.concatenate([lanes(head), lanes(lost0)], axis=1),
            jnp.concatenate([lanes(smooth), lanes(lost1)], axis=1),
        ],
        axis=0,
    )
    made = dot_tn(weights, stacked)
    span = blocks * tb
    for i in range(blocks):
        estimate = made[:, i * tb : (i + 1) * tb]
        recovered[i] = jnp.where(mine > 0.5, estimate, solution[i])
        residual[i] = right[i] - kept[i] - made[:, span + i * tb : span + (i + 1) * tb]


def reload_kernel(split_hbm, split, sems):
    blocks, pairs = split.shape[0], split.shape[1]
    chunk = pairs // 4
    copies = [
        pltpu.make_async_copy(
            split_hbm.at[row, k * chunk : (k + 1) * chunk],
            split.at[row, k * chunk : (k + 1) * chunk],
            sems.at[row, k],
        )
        for row in range(blocks)
        for k in range(4)
    ]
    for copy in copies:
        copy.start()
    for copy in copies:
        copy.wait()


def reload_call(split):
    return pl.pallas_call(
        reload_kernel,
        out_shape=jax.ShapeDtypeStruct(split.shape, split.dtype),
        in_specs=[spec(pltpu.HBM)],
        out_specs=spec(VMEM),
        scratch_shapes=[pltpu.SemaphoreType.DMA((split.shape[0], 4))],
        compiler_params=params(16),
        cost_estimate=pl.CostEstimate(flops=0, bytes_accessed=4 * split.size, transcendentals=0),
    )(split)


def small_call(kernel, outs, lost, gathered, *arrays):
    return pl.pallas_call(
        kernel,
        out_shape=outs,
        in_specs=[spec(SMEM)] + [spec(VMEM)] * (1 + len(arrays)),
        out_specs=[spec(VMEM)] * len(outs),
        compiler_params=params(16),
    )(lost, gathered, *arrays)


def move(value, where, inside=False):
    rows = lax.axis_size("row")
    total = rows * lax.axis_size("grp")
    pairs = [(i, where(i)) for i in range(total) if 0 <= where(i) < total]
    if inside:
        pairs = [(i, j) for i, j in pairs if i // rows == j // rows]
    return lax.ppermute(value, AXES, pairs)


def window(value, inside=False):
    swapped = move(value, lambda i: i ^ 1)
    pair = jnp.concatenate([value, swapped], axis=0)
    near = move(pair, lambda i: i - 1 if i % 2 == 0 else i + 1, inside)
    far = move(value, lambda i: i - 3 if i % 2 == 0 else i + 3, inside)
    other = move(near, lambda i: i ^ 1)
    return value, swapped, near, other, far


def exchange(gram):
    return lax.all_to_all(gram, AXES, 0, 0)


def per_device(matrix_tiles, column_index, precond, right_side, lost_group):
    blocks, cols, tb = right_side.shape
    assert -(-BAND // blocks) == REACH <= lax.axis_size("row")
    total = lax.axis_size("row") * lax.axis_size("grp")

    def shape(*lead):
        return jax.ShapeDtypeStruct((*lead, cols, tb), jnp.float32)

    vec, vec3 = shape(blocks), shape(3, blocks)
    gram = jax.ShapeDtypeStruct((total, cols // 2, 8 * cols), jnp.float32)
    assert tb == 8 * cols
    held = VMEM(right_side.shape, jnp.float32)
    placing = (column_index, lost_group)

    *split, halves, smooth_b = split_call(matrix_tiles, precond, right_side)
    parts_b, image, smooth_o = tile_call(
        first_kernel, 3, [vec3, vec, vec], [], split,
        (halves,) + window(right_side), *placing,
    )
    parts_y, gram_outer, smooth = tile_call(
        second_kernel, 3, [vec3, gram, shape(3 * blocks)], [held], split,
        (halves, smooth_b, smooth_o, right_side) + window(image), *placing,
    )
    around = window(smooth, inside=True)
    gathered = exchange(gram_outer)
    held_split = pltpu.with_memory_space_constraint(split[1], pltpu.HBM)
    (moved,) = tile_call(
        third_kernel, 3, [vec3],
        [VMEM(split[1].shape, split[1].dtype), pltpu.SemaphoreType.DMA((blocks - STAY,))],
        (split[0], held_split), around, *placing, place=pltpu.HBM,
    )
    solution, target, applied, kept, pair = small_call(
        outer_kernel, [vec] * 4 + [shape(2 * blocks)], lost_group, gathered, right_side, image,
        parts_b, parts_y, smooth, moved, halves,
    )
    split = (split[0], reload_call(held_split))
    lost0, lost1, gram_inner = tile_call(
        fourth_kernel, 3, [vec, vec, gram], [held], split,
        (target, applied) + window(pair), *placing,
    )
    recovered, residual = small_call(
        inner_kernel, [vec] * 2, lost_group, exchange(gram_inner), right_side, solution, kept, pair,
        lost0, lost1,
    )
    return (recovered, residual)


def solution(mesh):
    in_specs = (
        P(("grp", "row"), None, None, None),
        P(("grp", "row"), None),
        P(("grp", "row"), None, None),
        P(("grp", "row"), None, None),
        P(),
    )
    out_specs = (P(("grp", "row"), None, None), P(("grp", "row"), None, None))

    return jax.shard_map(
        per_device, mesh=mesh, in_specs=in_specs, out_specs=out_specs, check_vma=False
    )
```
